32 devices in a mesh: section: 4 (over y, x), expert: 8 (over z, core).
Axes of the slice: x: 2, y: 2, z: 4, core: 2. Of those that a mesh axis runs over, the one named last changes fastest.
Arguments:
- sent_fwd: bfloat16 [4, 512, 3584], P('section', 'expert'), may hold values from -6 to 6
- sent_bwd: bfloat16 [4, 512, 3584], P('section', 'expert'), may hold values from -6 to 6
- router_w: float32 [4, 3584, 4], P('section'), may hold values from -0.5 to 0.5
- w_up: bfloat16 [4, 3584, 4096], P('section', None, 'expert'), may hold values from -0.09375 to 0.09375
- w_down: bfloat16 [4, 4096, 3584], P('section', 'expert'), may hold values from -0.1875 to 0.1875
- routes_fwd: int32 [4, 512, 1], P('section', 'expert'), may hold values from 0 to 3; in each aligned block of 64 rows (0 to 63, 64 to 127, ..., all dimensions but the last counted through in order) at most 17 rows name the same one
- routes_bwd: int32 [4, 512, 1], P('section', 'expert'), may hold values from 0 to 3; in each aligned block of 64 rows (0 to 63, 64 to 127, ..., all dimensions but the last counted through in order) at most 17 rows name the same one
Outputs:
- out_fwd: bfloat16 [4, 512, 3584], P('section', 'expert')
- out_bwd: bfloat16 [4, 512, 3584], P('section', 'expert')
The draws below stay inside these ranges and needn't reach their ends.
Inputs may be any that keep to these rules, and one draw needn't show every extreme that they name: `routes_fwd`: at each section the 64 rows of one device name any one expert at most 17 times in all, a bound that some block reaches. `routes_bwd`: at each section the 64 rows of one device name any one expert at most 17 times in all, a bound that some block reaches.
All inputs are finite; a program needn't handle non-finite values.
Results may differ from the reference program's by a relative error of at most 0.003.
Values may be sent and summed in bfloat16 or wider, within the bound.
A program may use at most 128 MiB of HBM per device.

```python
import math
import jax
import jax.numpy as jnp
import numpy as np
from jax import lax

D = 3584
FF = 1024
EXPERTS = 4
TOPK = 1
TOK_DEV = 64
CAP = 17
SPLIT = 2
HID_DEV = 512
HID_ALL = 4096
SECTIONS = 4
TOKENS = 512
N_EXPERT = 8


def levels(rng, shape, pieces, least, top_value):
    gain, own = 1.0, jax.random.fold_in(rng, 6)
    for dim, shards_of in pieces:
        steps = jnp.exp(jax.random.uniform(jax.random.fold_in(own, dim), (shards_of,), jnp.float32, least / len(pieces), top_value / len(pieces)))
        gain = gain * jnp.repeat(steps, shape[dim] // shards_of).reshape([-1 if axis == dim else 1 for axis in range(len(shape))])
    return gain


def deal_out(key, own, number, rows, count, top, bound, slope):
    sequence = jax.random.permutation(key, count)
    heavy_load, ordinary = load_shares(count, rows * top, bound, slope, True), load_shares(count, rows * top, bound, slope, False)
    places = jnp.arange(count)

    def named(tallies, turn):
        used = int((tallies > 0).sum())
        fixed = max(1, used // 4)
        passed = fixed + (places - fixed + turn * (used - fixed)) % max(1, count - fixed)
        return jnp.zeros((count,), jnp.int32).at[sequence[jnp.where(places < fixed, places, passed)]].set(jnp.asarray(tallies, jnp.int32))

    tallies = jnp.where(number % 4 == 0, named(heavy_load, number // 4), named(ordinary, number - number // 4 - 1))
    mixed = jax.random.permutation(jax.random.fold_in(own, 3), count)
    giver, receiver = mixed[0:count // 2 * 2:2], mixed[1:count // 2 * 2:2]
    slack = jnp.minimum(tallies[giver] - 1, bound - tallies[receiver]) // 2
    slack = jnp.where((giver == sequence[0]) | (receiver == sequence[0]) | (tallies[receiver] == 0), 0, jnp.maximum(slack, 0))
    passed = jax.random.randint(jax.random.fold_in(own, 4), (count // 2,), 0, 1 << 20) % (slack + 1)
    tallies = tallies.at[giver].add(-passed).at[receiver].add(passed)
    labels = jnp.searchsorted(jnp.cumsum(tallies), jnp.arange(rows * top), side="right").astype(jnp.int32)
    listing = labels.reshape(top, rows).T
    listing = listing[jax.random.permutation(jax.random.fold_in(own, 1), rows)]
    turn = jax.random.randint(jax.random.fold_in(own, 2), (rows, 1), 0, top)
    return jnp.take_along_axis(listing, (jnp.arange(top)[None, :] + turn) % top, axis=1)


def load_shares(count, total, bound, skew, full):
    loads = [(1 << 20) // math.isqrt(rank ** skew) + 1 for rank in range(1, count + 1)]
    largest = bound if full else min(bound, max(-(-total // count), total * loads[0] // sum(loads)))
    least = 1 if total - largest >= count - 1 else 0
    given, rest = [largest] + [least] * (count - 1), total - largest - least * (count - 1)
    while rest > 0:
        candidates = [i for i in range(1, count) if given[i] < largest] or [i for i in range(1, count) if given[i] < bound]
        whole, remaining = sum([loads[i] for i in candidates]), rest
        for i in candidates:
            extra = min(bound - given[i], max(1, remaining * loads[i] // whole), rest)
            given[i] = given[i] + extra
            rest = rest - extra
    return np.array(given)


def bell_draw(key, dims, width, bound, cuts=(), kind=jnp.bfloat16):
    factor_of = levels(key, dims, cuts, -0.22, 0.18) if cuts else 1.0
    entries = jax.random.normal(key, dims, jnp.float32) * width * factor_of
    return jnp.minimum(jnp.maximum(entries, -bound), bound).astype(kind)


def setup_inputs(seed: int = 0) -> dict:
    streams_of = jax.random.split(jax.random.key(seed), 8)
    sent_fwd = bell_draw(streams_of[0], (SECTIONS, TOKENS, D), 1.0, 6.0, ((0, 4), (1, 8)))
    sent_bwd = bell_draw(streams_of[1], (SECTIONS, TOKENS, D), 1.0, 6.0, ((0, 4), (1, 8)))
    router_w = bell_draw(streams_of[2], (SECTIONS, D, EXPERTS), (2 * D ** -0.5), 0.5, ((0, 4),), jnp.float32)
    w_up = bell_draw(streams_of[3], (SECTIONS, D, HID_ALL), D ** -0.5, 0.09375, ((0, 4), (2, 8)))
    w_down = bell_draw(streams_of[4], (SECTIONS, HID_ALL, D), FF ** -0.5, 0.1875, ((0, 4), (1, 8)))
    routes_fwd_keys = jax.random.split(jax.random.fold_in(streams_of[5], 1), SECTIONS * TOKENS // TOK_DEV)
    routes_fwd_turns = jax.random.permutation(jax.random.fold_in(streams_of[5], 3), SECTIONS * TOKENS // TOK_DEV)
    routes_fwd = jax.vmap(lambda own, number: deal_out(jax.random.fold_in(streams_of[5], 2), own, number, TOK_DEV, EXPERTS, TOPK, CAP, 2))(routes_fwd_keys, routes_fwd_turns).reshape((SECTIONS, TOKENS, TOPK))
    routes_bwd_keys = jax.random.split(jax.random.fold_in(streams_of[6], 1), SECTIONS * TOKENS // TOK_DEV)
    routes_bwd_turns = jax.random.permutation(jax.random.fold_in(streams_of[6], 3), SECTIONS * TOKENS // TOK_DEV)
    routes_bwd = jax.vmap(lambda own, number: deal_out(jax.random.fold_in(streams_of[6], 2), own, number, TOK_DEV, EXPERTS, TOPK, CAP, 2))(routes_bwd_keys, routes_bwd_turns).reshape((SECTIONS, TOKENS, TOPK))
    return {"sent_fwd": sent_fwd, "sent_bwd": sent_bwd, "router_w": router_w, "w_up": w_up, "w_down": w_down, "routes_fwd": routes_fwd, "routes_bwd": routes_bwd}


def moe_layer(inputs, routes, router, up_weights, down_weights):
    chosen = routes.reshape(N_EXPERT, TOK_DEV * TOPK)
    onehot = (chosen[:, :, None] == jnp.arange(EXPERTS, dtype=jnp.int32)[None, None, :]).astype(jnp.int32)
    position = jnp.sum((jnp.cumsum(onehot, axis=1) - 1) * onehot, axis=2)
    source = jnp.arange(N_EXPERT, dtype=jnp.int32)[:, None]
    column = (source * CAP + position).reshape(-1).astype(jnp.int32)
    expert_of = chosen.reshape(-1).astype(jnp.int32)
    rows_in = jnp.repeat(inputs, TOPK, axis=0)
    buffer = jnp.zeros((EXPERTS, N_EXPERT * CAP, D), jnp.bfloat16).at[expert_of, column].set(rows_in)
    up_all = jnp.transpose(up_weights.reshape(D, EXPERTS, FF), (1, 0, 2))
    down_all = down_weights.reshape(EXPERTS, SPLIT, HID_DEV, D)

    def one_expert(operands):
        rows_here, up_expert, down_expert = operands
        hidden = jax.nn.silu(jnp.dot(rows_here, up_expert, preferred_element_type=jnp.float32)).astype(jnp.bfloat16)
        blocks = hidden.reshape(rows_here.shape[0], SPLIT, HID_DEV)
        summed = jnp.zeros((rows_here.shape[0], D), jnp.float32)
        for index_block in range(SPLIT):
            partial_out = jnp.dot(blocks[:, index_block], down_expert[index_block], preferred_element_type=jnp.float32).astype(jnp.bfloat16)
            partial_out = lax.optimization_barrier(partial_out)
            summed = summed + partial_out.astype(jnp.float32)
        return summed

    results = lax.map(one_expert, (buffer, up_all, down_all))
    gathered = results[expert_of, column].reshape(TOKENS, TOPK, D)
    logits = jnp.dot(inputs.astype(jnp.float32), router, precision=lax.Precision.HIGHEST)
    picked = jnp.take_along_axis(logits, routes, axis=1)
    scores = jax.nn.sigmoid(picked)
    mixed = inputs.astype(jnp.float32) + jnp.sum(scores[:, :, None] * gathered, axis=1)
    return mixed.astype(jnp.bfloat16)


def reference(sent_fwd, sent_bwd, router_w, w_up, w_down, routes_fwd, routes_bwd):
    inputs_fwd = jnp.roll(sent_fwd, 1, axis=0)
    inputs_bwd = jnp.roll(sent_bwd, -1, axis=0)

    def one_section(operands):
        first, second, route_first, route_second, router, up_weights, down_weights = operands
        return (moe_layer(first, route_first, router, up_weights, down_weights),
                moe_layer(second, route_second, router, up_weights, down_weights))

    out_fwd, out_bwd = lax.map(one_section, (inputs_fwd, inputs_bwd, routes_fwd, routes_bwd, router_w, w_up, w_down))
    return out_fwd, out_bwd
```

```python
import functools

import jax
import jax.numpy as jnp
from jax import lax
from jax.experimental import pallas as pl
from jax.experimental.pallas import tpu as pltpu
from jax.sharding import PartitionSpec as P

MESH = pl.DeviceIdType.MESH
F32 = jnp.float32
BF16 = jnp.bfloat16
NT = (((1,), (1,)), ((), ()))
BASE = 16
BLOCK = 256
CHUNK = 512


def iota(shape, dim):
    return lax.broadcasted_iota(jnp.int32, shape, dim)


def ones_where(mask):
    return jnp.where(mask, 1.0, 0.0).astype(BF16)


def exact(a, b):
    return jnp.dot(a, b, preferred_element_type=F32).astype(BF16)


def to_blocks(rows, number):
    height = rows[0].shape[0]
    i, j = iota((number * 16, len(rows) * height), 0), iota((number * 16, len(rows) * height), 1)
    take = ones_where(j == (i % 16) * height + i // 16)
    return exact(take, jnp.concatenate(rows, axis=0))


def from_blocks(blocks, number, height):
    n = blocks.shape[0]
    i, j = iota((number * height, n), 0), iota((number * height, n), 1)
    take = ones_where(i == (j % 16) * height + j // 16)
    rows = exact(take, blocks)
    return [rows[q * height:(q + 1) * height] for q in range(number)]


def positions(chosen, experts):
    tokens = chosen.shape[1]
    named = iota((16, tokens), 0) == chosen
    earlier = ones_where(iota((tokens, tokens), 0) < iota((tokens, tokens), 1))
    counted = jnp.dot(ones_where(named), earlier, preferred_element_type=F32)
    place = jnp.sum(jnp.where(named, counted, 0.0), axis=0, keepdims=True)
    return place.astype(jnp.int32)


def layer_kernel(
    dims,
    rf_hbm, rb_hbm, fwd_hbm, bwd_hbm, router_hbm, up_hbm, down_hbm,
    out_fwd, out_bwd,
    x_ref, rows_ref, pack_ref, up_ref, down_ref, hid_ref, router_ref, routes_ref, next_routes,
    part_out, part_in, own_part, y_ref, ret_ref,
    load_s, w_s, small_s, small_r, disp_s, disp_r, pair_s, pair_r, part_s, part_r, ret_s, ret_r, loc_s,
):
    chips, per_expert, experts, sections, tokens, width, hidden = dims
    blocks = width // BLOCK
    chunks = width // CHUNK
    main = chips * BASE
    spare = -(-chips // 16) * 16
    half = main + spare
    section = lax.axis_index("section")
    me = lax.axis_index("expert")
    core = lax.rem(me, 2)
    chip = me // 2
    sib = {"section": section, "expert": chip * 2 + 1 - core}
    after = lax.rem(section + 1, sections)
    before = lax.rem(section + sections - 1, sections)
    there = (after, before)

    def partner(v):
        other, bit = chip, 1
        while bit <= v:
            if (v // bit) % 2:
                other = other + bit - 2 * bit * lax.rem(chip // bit, 2)
            bit *= 2
        return other

    order = [v for v in range(chips // 2, chips)] + [v for v in range(1, chips // 2)] + [0]

    def remote(src, dst, send, recv, device):
        return pltpu.make_async_remote_copy(
            src_ref=src, dst_ref=dst, send_sem=send, recv_sem=recv,
            device_id=device, device_id_type=MESH,
        )

    def arrived(dst, send, recv):
        remote(dst, dst, send, recv, sib).wait_recv()

    loads = [
        pltpu.make_async_copy(rf_hbm, routes_ref.at[0], load_s.at[0]),
        pltpu.make_async_copy(rb_hbm, routes_ref.at[1], load_s.at[1]),
        pltpu.make_async_copy(fwd_hbm, x_ref.at[0], load_s.at[2]),
        pltpu.make_async_copy(bwd_hbm, x_ref.at[1], load_s.at[3]),
        pltpu.make_async_copy(router_hbm, router_ref, load_s.at[4]),
    ]
    for load in loads:
        load.start()
    w_up_copy = pltpu.make_async_copy(up_hbm, up_ref, w_s.at[0])
    w_down_copy = pltpu.make_async_copy(down_hbm, down_ref, w_s.at[1])

    barrier = pltpu.get_barrier_semaphore()
    greet = [sib]
    for s in there:
        greet.append({"section": s, "expert": me})
    for v in order[:-1]:
        greet.append({"section": section, "expert": partner(v) * 2 + core})
    for device in greet:
        pl.semaphore_signal(barrier, inc=1, device_id=device, device_id_type=MESH)
    loads[0].wait()
    loads[1].wait()
    pl.semaphore_wait(barrier, len(greet))

    sends = []

    def send(*args):
        copy = remote(*args)
        copy.start()
        sends.append(copy)

    for m in range(2):
        send(
            routes_ref.at[m], next_routes.at[m], small_s.at[m], small_r.at[m],
            {"section": there[1 - m], "expert": me},
        )
    w_up_copy.start()
    w_down_copy.start()

    for m in range(2):
        loads[2 + m].wait()
        arrived(next_routes.at[m], small_s.at[m], small_r.at[m])
        chosen = next_routes[m]
        place = positions(chosen, experts)
        slot = jnp.where(place < BASE, chosen * BASE + place, -1)
        slot = jnp.where(place >= BASE, experts * BASE + chosen, slot)
        take = ones_where(iota((experts * BASE + 16, tokens), 0) == slot)
        extra = []
        for k in range(chunks):
            packed = exact(take, x_ref[m, :, k * CHUNK:(k + 1) * CHUNK])
            pack_ref[m, :, k * CHUNK:(k + 1) * CHUNK] = packed[0:experts * BASE]
            for b in range(CHUNK // BLOCK):
                extra.append(packed[experts * BASE:, b * BLOCK:(b + 1) * BLOCK])
        pack_ref[m, :, width:] = to_blocks(extra, experts)
        for v in order:
            other = partner(v)
            send(
                pack_ref.at[m, pl.ds(pl.multiple_of(other // per_expert * BASE, BASE), BASE), :],
                rows_ref.at[m, pl.ds(v * BASE, BASE), :],
                disp_s.at[m, v], disp_r.at[m, v],
                {"section": there[m], "expert": other * 2 + core},
            )

    loads[4].wait()
    expert = chip // per_expert
    column = jnp.where(iota((experts, width), 0) == expert, router_ref[...], 0.0)
    column = jnp.sum(column, axis=0, keepdims=True)
    w_up_copy.wait()
    w_down_copy.wait()

    eye = ones_where(iota((tokens, tokens), 0) == iota((tokens, tokens), 1))
    unpack = []
    for m in range(2):
        chosen = routes_ref[m]
        place = positions(chosen, experts)
        picks = [
            ones_where((iota((BASE, tokens), 0) == place) & (chosen == d // per_expert)) for d in range(chips)
        ]
        row = iota((spare, tokens), 0)
        picks.append(ones_where((row // per_expert == chosen) & (row < chips) & (place >= BASE)))
        unpack.append(
            lax.dot_general(eye, jnp.concatenate(picks, axis=0), NT, preferred_element_type=F32).astype(BF16)
        )

    for m in range(2):
        for v in order:
            mine = rows_ref.at[m, pl.ds(v * BASE, BASE), :]
            arrived(mine, disp_s.at[m, v], disp_r.at[m, v])
            send(mine, rows_ref.at[m, pl.ds(half + v * BASE, BASE), :], pair_s.at[m, v], pair_r.at[m, v], sib)

        def spread(start):
            found = from_blocks(rows_ref[m, start:start + main, width:], blocks, spare)
            for q in range(blocks):
                rows_ref[m, start + main:start + half, q * BLOCK:(q + 1) * BLOCK] = found[q]

        spread(0)
        total = jnp.zeros((half, 128), F32)
        for b in range(width // 128):
            cols = slice(b * 128, (b + 1) * 128)
            total += rows_ref[m, 0:half, cols].astype(F32) * column[:, cols]
        score = jax.nn.sigmoid(jnp.sum(total, axis=1, keepdims=True))
        first = lax.rem(chip, per_expert) == 0

        for v in order:
            arrived(rows_ref.at[m, pl.ds(half + v * BASE, BASE), :], pair_s.at[m, v], pair_r.at[m, v])
        spread(half)
        hid_ref[m] = jax.nn.silu(
            jnp.dot(rows_ref[m, :, 0:width], up_ref[...], preferred_element_type=F32)
        ).astype(BF16)

        for k in range(chunks):
            part = exact(hid_ref[m], down_ref[:, k * CHUNK:(k + 1) * CHUNK])
            part_out[m, k] = part[half:]
            own_part[k] = part[0:half]
            send(part_out.at[m, k], part_in.at[m, k], part_s.at[m, k], part_r.at[m, k], sib)
        extra = []
        for k in range(chunks):
            arrived(part_in.at[m, k], part_s.at[m, k], part_r.at[m, k])
            added = score * (own_part[k].astype(F32) + part_in[m, k].astype(F32))
            x = rows_ref[m, 0:half, k * CHUNK:(k + 1) * CHUNK].astype(F32)
            if per_expert > 1:
                x = jnp.where(first, x, 0.0)
            y = (x + added).astype(BF16)
            y_ref[m, :, k * CHUNK:(k + 1) * CHUNK] = y[0:main]
            for b in range(CHUNK // BLOCK):
                extra.append(y[main:, b * BLOCK:(b + 1) * BLOCK])
        y_ref[m, :, width:] = to_blocks(extra, chips)
        for v in order:
            y = y_ref.at[m, pl.ds(v * BASE, BASE), :]
            home = ret_ref.at[m, pl.ds(pl.multiple_of(chip * BASE, BASE), BASE), :]
            if v == 0:
                local = pltpu.make_async_copy(y, home, loc_s.at[m])
                local.start()
            else:
                send(y, home, ret_s.at[m, v], ret_r.at[m, v], {"section": section, "expert": partner(v) * 2 + core})

    for m, out in enumerate((out_fwd, out_bwd)):
        for v in order:
            here = ret_ref.at[m, pl.ds(pl.multiple_of(partner(v) * BASE, BASE), BASE), :]
            if v == 0:
                pltpu.make_async_copy(here, here, loc_s.at[m]).wait()
            else:
                arrived(here, ret_s.at[m, v], ret_r.at[m, v])
        extra = from_blocks(ret_ref[m, :, width:], blocks, spare)
        for k in range(chunks):
            found = jnp.concatenate(extra[k * CHUNK // BLOCK:(k + 1) * CHUNK // BLOCK], axis=1)
            came = jnp.concatenate([ret_ref[m, :, k * CHUNK:(k + 1) * CHUNK], found], axis=0)
            out[:, k * CHUNK:(k + 1) * CHUNK] = exact(unpack[m], came)

    for copy in sends:
        copy.wait_send()


def write_kernel(a_ref, b_ref, out_a, out_b, sems):
    stores = [
        pltpu.make_async_copy(src, dst, sems.at[i]) for i, (src, dst) in enumerate(((a_ref, out_a), (b_ref, out_b)))
    ]
    for store in stores:
        store.start()
    for store in stores:
        store.wait()


def on_device(sent_fwd, sent_bwd, router_w, w_up, w_down, routes_fwd, routes_bwd):
    tokens, width = sent_fwd.shape[1:]
    hidden = w_up.shape[2]
    experts = router_w.shape[2]
    sections = lax.axis_size("section")
    chips = lax.axis_size("expert") // 2
    per_expert = chips // experts
    dims = (chips, per_expert, experts, sections, tokens, width, hidden)
    chunks = width // CHUNK
    wide = width + BLOCK
    main = chips * BASE
    half = main + -(-chips // 16) * 16
    dma = pltpu.SemaphoreType.DMA
    hbm = pl.BlockSpec(memory_space=pltpu.HBM)
    vmem = pl.BlockSpec(memory_space=pltpu.VMEM)
    shape = jax.ShapeDtypeStruct((tokens, width), BF16)
    out_fwd, out_bwd = pl.pallas_call(
        functools.partial(layer_kernel, dims),
        out_shape=(shape, shape),
        in_specs=[hbm] * 7,
        out_specs=(vmem, vmem),
        scratch_shapes=[
            pltpu.VMEM((2, tokens, width), BF16),
            pltpu.VMEM((2, 2 * half, wide), BF16),
            pltpu.VMEM((2, experts * BASE, wide), BF16),
            pltpu.VMEM((width, hidden), BF16),
            pltpu.VMEM((hidden, width), BF16),
            pltpu.VMEM((2, 2 * half, hidden), BF16),
            pltpu.VMEM((experts, width), F32),
            pltpu.VMEM((2, 1, tokens), jnp.int32),
            pltpu.VMEM((2, 1, tokens), jnp.int32),
            pltpu.VMEM((2, chunks, half, CHUNK), BF16),
            pltpu.VMEM((2, chunks, half, CHUNK), BF16),
            pltpu.VMEM((chunks, half, CHUNK), BF16),
            pltpu.VMEM((2, main, wide), BF16),
            pltpu.VMEM((2, main, wide), BF16),
            dma((5,)), dma((2,)), dma((2,)), dma((2,)),
            dma((2, chips)), dma((2, chips)),
            dma((2, chips)), dma((2, chips)),
            dma((2, chunks)), dma((2, chunks)),
            dma((2, chips)), dma((2, chips)), dma((2,)),
        ],
        compiler_params=pltpu.CompilerParams(
            collective_id=0, has_side_effects=True, vmem_limit_bytes=62 << 20
        ),
    )(
        routes_fwd.reshape(1, tokens), routes_bwd.reshape(1, tokens),
        sent_fwd[0], sent_bwd[0], router_w[0].T, w_up[0], w_down[0],
    )
    out_fwd, out_bwd = pl.pallas_call(
        write_kernel,
        out_shape=(shape, shape),
        in_specs=[vmem, vmem],
        out_specs=(hbm, hbm),
        scratch_shapes=[dma((2,))],
        compiler_params=pltpu.CompilerParams(has_side_effects=True, vmem_limit_bytes=8 << 20),
    )(out_fwd, out_bwd)
    return out_fwd[None], out_bwd[None]


def solution(mesh):
    return jax.shard_map(
        on_device,
        mesh=mesh,
        in_specs=(
            P("section", "expert", None),
            P("section", "expert", None),
            P("section", None, None),
            P("section", None, "expert"),
            P("section", "expert", None),
            P("section", "expert", None),
            P("section", "expert", None),
        ),
        out_specs=(P("section", "expert", None), P("section", "expert", None)),
        check_vma=False,
    )
```

```python
import functools

import jax
import jax.numpy as jnp
from jax import lax
from jax.experimental import pallas as pl
from jax.experimental.pallas import tpu as pltpu
from jax.sharding import PartitionSpec as P

MESH = pl.DeviceIdType.MESH
F32 = jnp.float32
BF16 = jnp.bfloat16
NT = (((1,), (1,)), ((), ()))
BASE = 16
BLOCK = 256
CHUNK = 512


def iota(shape, dim):
    return lax.broadcasted_iota(jnp.int32, shape, dim)


def ones_where(mask):
    return jnp.where(mask, 1.0, 0.0).astype(BF16)


def exact(a, b):
    return jnp.dot(a, b, preferred_element_type=F32).astype(BF16)


def to_blocks(rows, number):
    height = rows[0].shape[0]
    i, j = iota((number * 16, len(rows) * height), 0), iota((number * 16, len(rows) * height), 1)
    take = ones_where(j == (i % 16) * height + i // 16)
    return exact(take, jnp.concatenate(rows, axis=0))


def from_blocks(blocks, number, height):
    n = blocks.shape[0]
    i, j = iota((number * height, n), 0), iota((number * height, n), 1)
    take = ones_where(i == (j % 16) * height + j // 16)
    rows = exact(take, blocks)
    return [rows[q * height:(q + 1) * height] for q in range(number)]


def positions(chosen, experts):
    tokens = chosen.shape[1]
    named = iota((16, tokens), 0) == chosen
    earlier = ones_where(iota((tokens, tokens), 0) < iota((tokens, tokens), 1))
    counted = jnp.dot(ones_where(named), earlier, preferred_element_type=F32)
    place = jnp.sum(jnp.where(named, counted, 0.0), axis=0, keepdims=True)
    return place.astype(jnp.int32)


def layer_kernel(
    dims,
    rf_hbm, rb_hbm, fwd_hbm, bwd_hbm, router_hbm, up_hbm, down_hbm,
    out_fwd, out_bwd,
    x_ref, rows_ref, pack_ref, up_ref, down_ref, hid_ref, router_ref, routes_ref, next_routes,
    part_out, part_in, own_part, y_ref, ret_ref,
    load_s, w_s, small_s, small_r, disp_s, disp_r, pair_s, pair_r, part_s, part_r, ret_s, ret_r, loc_s,
):
    chips, per_expert, experts, sections, tokens, width, hidden = dims
    blocks = width // BLOCK
    chunks = width // CHUNK
    main = chips * BASE
    spare = -(-chips // 16) * 16
    half = main + spare
    section = lax.axis_index("section")
    me = lax.axis_index("expert")
    core = lax.rem(me, 2)
    chip = me // 2
    sib = {"section": section, "expert": chip * 2 + 1 - core}
    after = lax.rem(section + 1, sections)
    before = lax.rem(section + sections - 1, sections)
    there = (after, before)

    def partner(v):
        other, bit = chip, 1
        while bit <= v:
            if (v // bit) % 2:
                other = other + bit - 2 * bit * lax.rem(chip // bit, 2)
            bit *= 2
        return other

    order = [v for v in range(chips // 2, chips)] + [v for v in range(1, chips // 2)] + [0]

    def remote(src, dst, send, recv, device):
        return pltpu.make_async_remote_copy(
            src_ref=src, dst_ref=dst, send_sem=send, recv_sem=recv,
            device_id=device, device_id_type=MESH,
        )

    def arrived(dst, send, recv):
        remote(dst, dst, send, recv, sib).wait_recv()

    loads = [
        pltpu.make_async_copy(rf_hbm, routes_ref.at[0], load_s.at[0]),
        pltpu.make_async_copy(rb_hbm, routes_ref.at[1], load_s.at[1]),
        pltpu.make_async_copy(fwd_hbm, x_ref.at[0], load_s.at[2]),
        pltpu.make_async_copy(bwd_hbm, x_ref.at[1], load_s.at[3]),
        pltpu.make_async_copy(router_hbm, router_ref, load_s.at[4]),
    ]
    for load in loads:
        load.start()
    w_up_copy = pltpu.make_async_copy(up_hbm, up_ref, w_s.at[0])
    w_down_copy = pltpu.make_async_copy(down_hbm, down_ref, w_s.at[1])

    barrier = pltpu.get_barrier_semaphore()
    greet = [sib]
    for s in there:
        greet.append({"section": s, "expert": me})
    for v in order[:-1]:
        greet.append({"section": section, "expert": partner(v) * 2 + core})
    for device in greet:
        pl.semaphore_signal(barrier, inc=1, device_id=device, device_id_type=MESH)
    loads[0].wait()
    loads[1].wait()
    pl.semaphore_wait(barrier, len(greet))

    sends = []

    def send(*args):
        copy = remote(*args)
        copy.start()
        sends.append(copy)

    for m in range(2):
        send(
            routes_ref.at[m], next_routes.at[m], small_s.at[m], small_r.at[m],
            {"section": there[1 - m], "expert": me},
        )
    w_up_copy.start()
    w_down_copy.start()

    for m in range(2):
        loads[2 + m].wait()
        arrived(next_routes.at[m], small_s.at[m], small_r.at[m])
        chosen = next_routes[m]
        place = positions(chosen, experts)
        slot = jnp.where(place < BASE, chosen * BASE + place, -1)
        slot = jnp.where(place >= BASE, experts * BASE + chosen, slot)
        take = ones_where(iota((experts * BASE + 16, tokens), 0) == slot)
        extra = []
        for k in range(chunks):
            packed = exact(take, x_ref[m, :, k * CHUNK:(k + 1) * CHUNK])
            pack_ref[m, :, k * CHUNK:(k + 1) * CHUNK] = packed[0:experts * BASE]
            for b in range(CHUNK // BLOCK):
                extra.append(packed[experts * BASE:, b * BLOCK:(b + 1) * BLOCK])
        pack_ref[m, :, width:] = to_blocks(extra, experts)
        for v in order:
            other = partner(v)
            send(
                pack_ref.at[m, pl.ds(pl.multiple_of(other // per_expert * BASE, BASE), BASE), :],
                rows_ref.at[m, pl.ds(v * BASE, BASE), :],
                disp_s.at[m, v], disp_r.at[m, v],
                {"section": there[m], "expert": other * 2 + core},
            )

    loads[4].wait()
    expert = chip // per_expert
    column = jnp.where(iota((experts, width), 0) == expert, router_ref[...], 0.0)
    column = jnp.sum(column, axis=0, keepdims=True)
    w_up_copy.wait()
    w_down_copy.wait()

    eye = ones_where(iota((tokens, tokens), 0) == iota((tokens, tokens), 1))
    unpack = []
    for m in range(2):
        chosen = routes_ref[m]
        place = positions(chosen, experts)
        picks = [
            ones_where((iota((BASE, tokens), 0) == place) & (chosen == d // per_expert)) for d in range(chips)
        ]
        row = iota((spare, tokens), 0)
        picks.append(ones_where((row // per_expert == chosen) & (row < chips) & (place >= BASE)))
        unpack.append(
            lax.dot_general(eye, jnp.concatenate(picks, axis=0), NT, preferred_element_type=F32).astype(BF16)
        )

    for m in range(2):
        for v in order:
            mine = rows_ref.at[m, pl.ds(v * BASE, BASE), :]
            arrived(mine, disp_s.at[m, v], disp_r.at[m, v])
            send(mine, rows_ref.at[m, pl.ds(half + v * BASE, BASE), :], pair_s.at[m, v], pair_r.at[m, v], sib)

        def spread(start):
            found = from_blocks(rows_ref[m, start:start + main, width:], blocks, spare)
            for q in range(blocks):
                rows_ref[m, start + main:start + half, q * BLOCK:(q + 1) * BLOCK] = found[q]

        spread(0)
        total = jnp.zeros((half, 128), F32)
        for b in range(width // 128):
            cols = slice(b * 128, (b + 1) * 128)
            total += rows_ref[m, 0:half, cols].astype(F32) * column[:, cols]
        score = jax.nn.sigmoid(jnp.sum(total, axis=1, keepdims=True))
        first = lax.rem(chip, per_expert) == 0

        for v in order:
            arrived(rows_ref.at[m, pl.ds(half + v * BASE, BASE), :], pair_s.at[m, v], pair_r.at[m, v])
        spread(half)
        hid_ref[m] = jax.nn.silu(
            jnp.dot(rows_ref[m, :, 0:width], up_ref[...], preferred_element_type=F32)
        ).astype(BF16)

        for k in range(chunks):
            part = exact(hid_ref[m], down_ref[:, k * CHUNK:(k + 1) * CHUNK])
            part_out[m, k] = part[half:]
            own_part[k] = part[0:half]
            send(part_out.at[m, k], part_in.at[m, k], part_s.at[m, k], part_r.at[m, k], sib)
        extra = []
        for k in range(chunks):
            arrived(part_in.at[m, k], part_s.at[m, k], part_r.at[m, k])
            added = score * (own_part[k].astype(F32) + part_in[m, k].astype(F32))
            x = rows_ref[m, 0:half, k * CHUNK:(k + 1) * CHUNK].astype(F32)
            if per_expert > 1:
                x = jnp.where(first, x, 0.0)
            y = (x + added).astype(BF16)
            y_ref[m, :, k * CHUNK:(k + 1) * CHUNK] = y[0:main]
            for b in range(CHUNK // BLOCK):
                extra.append(y[main:, b * BLOCK:(b + 1) * BLOCK])
        y_ref[m, :, width:] = to_blocks(extra, chips)
        for v in order:
            y = y_ref.at[m, pl.ds(v * BASE, BASE), :]
            home = ret_ref.at[m, pl.ds(pl.multiple_of(chip * BASE, BASE), BASE), :]
            if v == 0:
                local = pltpu.make_async_copy(y, home, loc_s.at[m])
                local.start()
            else:
                send(y, home, ret_s.at[m, v], ret_r.at[m, v], {"section": section, "expert": partner(v) * 2 + core})

    for m, out in enumerate((out_fwd, out_bwd)):
        for v in order:
            here = ret_ref.at[m, pl.ds(pl.multiple_of(partner(v) * BASE, BASE), BASE), :]
            if v == 0:
                pltpu.make_async_copy(here, here, loc_s.at[m]).wait()
            else:
                arrived(here, ret_s.at[m, v], ret_r.at[m, v])
        extra = from_blocks(ret_ref[m, :, width:], blocks, spare)
        for k in range(chunks):
            found = jnp.concatenate(extra[k * CHUNK // BLOCK:(k + 1) * CHUNK // BLOCK], axis=1)
            came = jnp.concatenate([ret_ref[m, :, k * CHUNK:(k + 1) * CHUNK], found], axis=0)
            out[:, k * CHUNK:(k + 1) * CHUNK] = exact(unpack[m], came)

    for copy in sends:
        copy.wait_send()


def write_kernel(a_ref, b_ref, out_a, out_b, sems):
    stores = [
        pltpu.make_async_copy(src, dst, sems.at[i]) for i, (src, dst) in enumerate(((a_ref, out_a), (b_ref, out_b)))
    ]
    for store in stores:
        store.start()
    for store in stores:
        store.wait()


def on_device(sent_fwd, sent_bwd, router_w, w_up, w_down, routes_fwd, routes_bwd):
    tokens, width = sent_fwd.shape[1:]
    hidden = w_up.shape[2]
    experts = router_w.shape[2]
    sections = lax.axis_size("section")
    chips = lax.axis_size("expert") // 2
    per_expert = chips // experts
    dims = (chips, per_expert, experts, sections, tokens, width, hidden)
    chunks = width // CHUNK
    wide = width + BLOCK
    main = chips * BASE
    half = main + -(-chips // 16) * 16
    dma = pltpu.SemaphoreType.DMA
    hbm = pl.BlockSpec(memory_space=pltpu.HBM)
    vmem = pl.BlockSpec(memory_space=pltpu.VMEM)
    shape = jax.ShapeDtypeStruct((tokens, width), BF16)
    out_fwd, out_bwd = pl.pallas_call(
        functools.partial(layer_kernel, dims),
        out_shape=(shape, shape),
        in_specs=[hbm] * 7,
        out_specs=(vmem, vmem),
        scratch_shapes=[
            pltpu.VMEM((2, tokens, width), BF16),
            pltpu.VMEM((2, 2 * half, wide), BF16),
            pltpu.VMEM((2, experts * BASE, wide), BF16),
            pltpu.VMEM((width, hidden), BF16),
            pltpu.VMEM((hidden, width), BF16),
            pltpu.VMEM((2, 2 * half, hidden), BF16),
            pltpu.VMEM((experts, width), F32),
            pltpu.VMEM((2, 1, tokens), jnp.int32),
            pltpu.VMEM((2, 1, tokens), jnp.int32),
            pltpu.VMEM((2, chunks, half, CHUNK), BF16),
            pltpu.VMEM((2, chunks, half, CHUNK), BF16),
            pltpu.VMEM((chunks, half, CHUNK), BF16),
            pltpu.VMEM((2, main, wide), BF16),
            pltpu.VMEM((2, main, wide), BF16),
            dma((5,)), dma((2,)), dma((2,)), dma((2,)),
            dma((2, chips)), dma((2, chips)),
            dma((2, chips)), dma((2, chips)),
            dma((2, chunks)), dma((2, chunks)),
            dma((2, chips)), dma((2, chips)), dma((2,)),
        ],
        compiler_params=pltpu.CompilerParams(
            collective_id=0, has_side_effects=True, vmem_limit_bytes=40 << 20
        ),
    )(
        *[pltpu.with_memory_space_constraint(given, pltpu.HBM) for given in (
            routes_fwd.reshape(1, tokens), routes_bwd.reshape(1, tokens),
            sent_fwd[0], sent_bwd[0], router_w[0].T, w_up[0], w_down[0],
        )]
    )
    out_fwd, out_bwd = pl.pallas_call(
        write_kernel,
        out_shape=(shape, shape),
        in_specs=[vmem, vmem],
        out_specs=(hbm, hbm),
        scratch_shapes=[dma((2,))],
        compiler_params=pltpu.CompilerParams(has_side_effects=True, vmem_limit_bytes=8 << 20),
    )(out_fwd, out_bwd)
    return out_fwd[None], out_bwd[None]


def solution(mesh):
    return jax.shard_map(
        on_device,
        mesh=mesh,
        in_specs=(
            P("section", "expert", None),
            P("section", "expert", None),
            P("section", None, None),
            P("section", None, "expert"),
            P("section", "expert", None),
            P("section", "expert", None),
            P("section", "expert", None),
        ),
        out_specs=(P("section", "expert", None), P("section", "expert", None)),
        check_vma=False,
    )
```

```python
import functools

import jax
import jax.numpy as jnp
from jax import lax
from jax.experimental import pallas as pl
from jax.experimental.pallas import tpu as pltpu
from jax.sharding import PartitionSpec as P

MESH = pl.DeviceIdType.MESH
F32 = jnp.float32
BF16 = jnp.bfloat16
NT = (((1,), (1,)), ((), ()))
BASE = 16
BLOCK = 256
CHUNK = 512


def iota(shape, dim):
    return lax.broadcasted_iota(jnp.int32, shape, dim)


def ones_where(mask):
    return jnp.where(mask, 1.0, 0.0).astype(BF16)


def exact(a, b):
    return jnp.dot(a, b, preferred_element_type=F32).astype(BF16)


def to_blocks(rows, number):
    height = rows[0].shape[0]
    i, j = iota((number * 16, len(rows) * height), 0), iota((number * 16, len(rows) * height), 1)
    take = ones_where(j == (i % 16) * height + i // 16)
    return exact(take, jnp.concatenate(rows, axis=0))


def from_blocks(blocks, number, height):
    n = blocks.shape[0]
    i, j = iota((number * height, n), 0), iota((number * height, n), 1)
    take = ones_where(i == (j % 16) * height + j // 16)
    rows = exact(take, blocks)
    return [rows[q * height:(q + 1) * height] for q in range(number)]


def positions(chosen, experts):
    tokens = chosen.shape[1]
    named = iota((16, tokens), 0) == chosen
    earlier = ones_where(iota((tokens, tokens), 0) < iota((tokens, tokens), 1))
    counted = jnp.dot(ones_where(named), earlier, preferred_element_type=F32)
    place = jnp.sum(jnp.where(named, counted, 0.0), axis=0, keepdims=True)
    return place.astype(jnp.int32)


def slots(chosen, experts):
    place = positions(chosen, experts)
    return jnp.where(place < BASE, chosen * BASE + place, experts * BASE + chosen)


def layer_kernel(
    dims,
    rf_hbm, rb_hbm, fwd_hbm, bwd_hbm, router_hbm, up_hbm, down_hbm,
    out_fwd, out_bwd,
    x_ref, rows_ref, pack_ref, up_ref, down_ref, hid_ref, router_ref, routes_ref, slot_ref, next_slots,
    part_out, part_in, own_part, y_ref, ret_ref,
    load_s, w_s, small_s, small_r, disp_s, disp_r, pair_s, pair_r, part_s, part_r, ret_s, ret_r, loc_s, chain, far,
):
    chips, per_expert, experts, sections, tokens, width, hidden = dims
    blocks = width // BLOCK
    chunks = width // CHUNK
    main = chips * BASE
    spare = -(-chips // 16) * 16
    half = main + spare
    section = lax.axis_index("section")
    me = lax.axis_index("expert")
    core = lax.rem(me, 2)
    chip = me // 2
    sib = {"section": section, "expert": chip * 2 + 1 - core}
    after = lax.rem(section + 1, sections)
    before = lax.rem(section + sections - 1, sections)
    there = (after, before)

    def partner(v):
        other, bit = chip, 1
        while bit <= v:
            if (v // bit) % 2:
                other = other + bit - 2 * bit * lax.rem(chip // bit, 2)
            bit *= 2
        return other

    def beside(v):
        return (partner(v) == chip + 1) | (partner(v) == chip - 1)

    order = [v for v in range(chips // 2, chips)] + [v for v in range(1, chips // 2)] + [0]

    def remote(src, dst, send, recv, device):
        return pltpu.make_async_remote_copy(
            src_ref=src, dst_ref=dst, send_sem=send, recv_sem=recv,
            device_id=device, device_id_type=MESH,
        )

    def arrived(dst, send, recv):
        remote(dst, dst, send, recv, sib).wait_recv()

    above = {"section": section, "expert": me + 2}
    below = {"section": section, "expert": me - 2}
    inner = (chip >= 1) & (chip <= chips - 2)

    def signal(semaphore, device):
        pl.semaphore_signal(semaphore, inc=1, device_id=device, device_id_type=MESH)

    barrier = pltpu.get_barrier_semaphore()
    for s in there:
        signal(barrier, {"section": s, "expert": me})
    signal(barrier, sib)

    @pl.when(chip > 0)
    def _():
        signal(barrier, below)

    @pl.when(chip < chips - 1)
    def _():
        signal(barrier, above)

    loads = [
        pltpu.make_async_copy(rf_hbm, routes_ref.at[0], load_s.at[0]),
        pltpu.make_async_copy(rb_hbm, routes_ref.at[1], load_s.at[1]),
        pltpu.make_async_copy(fwd_hbm, x_ref.at[0], load_s.at[2]),
        pltpu.make_async_copy(bwd_hbm, x_ref.at[1], load_s.at[3]),
        pltpu.make_async_copy(router_hbm, router_ref, load_s.at[4]),
    ]
    for load in loads:
        load.start()
    w_up_copy = pltpu.make_async_copy(up_hbm, up_ref, w_s.at[0])
    w_down_copy = pltpu.make_async_copy(down_hbm, down_ref, w_s.at[1])
    for m in range(2):
        loads[m].wait()
        slot_ref[m] = slots(routes_ref[m], experts)
    pl.semaphore_wait(barrier, 3 + jnp.where(chip > 0, 1, 0) + jnp.where(chip < chips - 1, 1, 0))

    sends = []

    def send(*args):
        copy = remote(*args)
        copy.start()
        sends.append(copy)

    for m in range(2):
        send(
            slot_ref.at[m], next_slots.at[m], small_s.at[m], small_r.at[m],
            {"section": there[1 - m], "expert": me},
        )

    @pl.when(chip >= 2)
    def _():
        pl.semaphore_wait(chain.at[0], 1)

    @pl.when(inner)
    def _():
        signal(chain.at[0], above)

    @pl.when(chip <= chips - 3)
    def _():
        pl.semaphore_wait(chain.at[1], 1)

    @pl.when(inner)
    def _():
        signal(chain.at[1], below)

    for m in range(2):
        signal(far.at[m], {"section": there[1 - m], "expert": me})
    w_up_copy.start()
    w_down_copy.start()

    for m in range(2):
        loads[2 + m].wait()
        arrived(next_slots.at[m], small_s.at[m], small_r.at[m])
        take = ones_where(iota((experts * BASE + 16, tokens), 0) == next_slots[m])
        extra = []
        for k in range(chunks):
            packed = exact(take, x_ref[m, :, k * CHUNK:(k + 1) * CHUNK])
            pack_ref[m, :, k * CHUNK:(k + 1) * CHUNK] = packed[0:experts * BASE]
            for b in range(CHUNK // BLOCK):
                extra.append(packed[experts * BASE:, b * BLOCK:(b + 1) * BLOCK])
        pack_ref[m, :, width:] = to_blocks(extra, experts)
        copies = {}
        for v in order:
            other = partner(v)
            copies[v] = remote(
                pack_ref.at[m, pl.ds(pl.multiple_of(other // per_expert * BASE, BASE), BASE), :],
                rows_ref.at[m, pl.ds(v * BASE, BASE), :],
                disp_s.at[m, v], disp_r.at[m, v],
                {"section": there[m], "expert": other * 2 + core},
            )
            sends.append(copies[v])
        if m == 0:
            for v in order:
                if v in (0, 1):
                    copies[v].start()
                elif v & (v + 1) == 0:
                    pl.when(beside(v))(copies[v].start)
        pl.semaphore_wait(far.at[m], 1)
        for v in order:
            if m == 1 or v & (v + 1):
                copies[v].start()
            elif v > 1:
                pl.when(jnp.logical_not(beside(v)))(copies[v].start)

    loads[4].wait()
    expert = chip // per_expert
    column = jnp.where(iota((experts, width), 0) == expert, router_ref[...], 0.0)
    column = jnp.sum(column, axis=0, keepdims=True)
    w_up_copy.wait()
    w_down_copy.wait()

    eye = ones_where(iota((tokens, tokens), 0) == iota((tokens, tokens), 1))
    unpack = []
    for m in range(2):
        slot = slot_ref[m]
        picks = [ones_where(iota((BASE, tokens), 0) == slot - d // per_expert * BASE) for d in range(chips)]
        row = iota((spare, tokens), 0)
        picks.append(ones_where((row // per_expert == slot - experts * BASE) & (row < chips)))
        unpack.append(
            lax.dot_general(eye, jnp.concatenate(picks, axis=0), NT, preferred_element_type=F32).astype(BF16)
        )

    for m in range(2):
        for v in order:
            mine = rows_ref.at[m, pl.ds(v * BASE, BASE), :]
            arrived(mine, disp_s.at[m, v], disp_r.at[m, v])
            send(mine, rows_ref.at[m, pl.ds(half + v * BASE, BASE), :], pair_s.at[m, v], pair_r.at[m, v], sib)

        def spread(start):
            found = from_blocks(rows_ref[m, start:start + main, width:], blocks, spare)
            for q in range(blocks):
                rows_ref[m, start + main:start + half, q * BLOCK:(q + 1) * BLOCK] = found[q]

        spread(0)
        total = jnp.zeros((half, 128), F32)
        for b in range(width // 128):
            cols = slice(b * 128, (b + 1) * 128)
            total += rows_ref[m, 0:half, cols].astype(F32) * column[:, cols]
        score = jax.nn.sigmoid(jnp.sum(total, axis=1, keepdims=True))
        first = lax.rem(chip, per_expert) == 0

        for v in order:
            arrived(rows_ref.at[m, pl.ds(half + v * BASE, BASE), :], pair_s.at[m, v], pair_r.at[m, v])
        spread(half)
        hid_ref[m] = jax.nn.silu(
            jnp.dot(rows_ref[m, :, 0:width], up_ref[...], preferred_element_type=F32)
        ).astype(BF16)

        for k in range(chunks):
            part = exact(hid_ref[m], down_ref[:, k * CHUNK:(k + 1) * CHUNK])
            part_out[m, k] = part[half:]
            own_part[k] = part[0:half]
            send(part_out.at[m, k], part_in.at[m, k], part_s.at[m, k], part_r.at[m, k], sib)
        extra = []
        for k in range(chunks):
            arrived(part_in.at[m, k], part_s.at[m, k], part_r.at[m, k])
            added = score * (own_part[k].astype(F32) + part_in[m, k].astype(F32))
            x = rows_ref[m, 0:half, k * CHUNK:(k + 1) * CHUNK].astype(F32)
            if per_expert > 1:
                x = jnp.where(first, x, 0.0)
            y = (x + added).astype(BF16)
            y_ref[m, :, k * CHUNK:(k + 1) * CHUNK] = y[0:main]
            for b in range(CHUNK // BLOCK):
                extra.append(y[main:, b * BLOCK:(b + 1) * BLOCK])
        y_ref[m, :, width:] = to_blocks(extra, chips)
        for v in order:
            y = y_ref.at[m, pl.ds(v * BASE, BASE), :]
            home = ret_ref.at[m, pl.ds(pl.multiple_of(chip * BASE, BASE), BASE), :]
            if v == 0:
                local = pltpu.make_async_copy(y, home, loc_s.at[m])
                local.start()
            else:
                send(y, home, ret_s.at[m, v], ret_r.at[m, v], {"section": section, "expert": partner(v) * 2 + core})

    for m, out in enumerate((out_fwd, out_bwd)):
        for v in order:
            here = ret_ref.at[m, pl.ds(pl.multiple_of(partner(v) * BASE, BASE), BASE), :]
            if v == 0:
                pltpu.make_async_copy(here, here, loc_s.at[m]).wait()
            else:
                arrived(here, ret_s.at[m, v], ret_r.at[m, v])
        extra = from_blocks(ret_ref[m, :, width:], blocks, spare)
        for k in range(chunks):
            found = jnp.concatenate(extra[k * CHUNK // BLOCK:(k + 1) * CHUNK // BLOCK], axis=1)
            came = jnp.concatenate([ret_ref[m, :, k * CHUNK:(k + 1) * CHUNK], found], axis=0)
            out[:, k * CHUNK:(k + 1) * CHUNK] = exact(unpack[m], came)

    for copy in sends:
        copy.wait_send()


def write_kernel(a_ref, b_ref, out_a, out_b, sems):
    stores = [
        pltpu.make_async_copy(src, dst, sems.at[i]) for i, (src, dst) in enumerate(((a_ref, out_a), (b_ref, out_b)))
    ]
    for store in stores:
        store.start()
    for store in stores:
        store.wait()


def on_device(sent_fwd, sent_bwd, router_w, w_up, w_down, routes_fwd, routes_bwd):
    tokens, width = sent_fwd.shape[1:]
    hidden = w_up.shape[2]
    experts = router_w.shape[2]
    sections = lax.axis_size("section")
    chips = lax.axis_size("expert") // 2
    per_expert = chips // experts
    dims = (chips, per_expert, experts, sections, tokens, width, hidden)
    chunks = width // CHUNK
    wide = width + BLOCK
    main = chips * BASE
    half = main + -(-chips // 16) * 16
    dma = pltpu.SemaphoreType.DMA
    hbm = pl.BlockSpec(memory_space=pltpu.HBM)
    vmem = pl.BlockSpec(memory_space=pltpu.VMEM)
    shape = jax.ShapeDtypeStruct((tokens, width), BF16)
    out_fwd, out_bwd = pl.pallas_call(
        functools.partial(layer_kernel, dims),
        out_shape=(shape, shape),
        in_specs=[hbm] * 7,
        out_specs=(vmem, vmem),
        scratch_shapes=[
            pltpu.VMEM((2, tokens, width), BF16),
            pltpu.VMEM((2, 2 * half, wide), BF16),
            pltpu.VMEM((2, experts * BASE, wide), BF16),
            pltpu.VMEM((width, hidden), BF16),
            pltpu.VMEM((hidden, width), BF16),
            pltpu.VMEM((2, 2 * half, hidden), BF16),
            pltpu.VMEM((experts, width), F32),
            pltpu.VMEM((2, 1, tokens), jnp.int32),
            pltpu.VMEM((2, 1, tokens), jnp.int32),
            pltpu.VMEM((2, 1, tokens), jnp.int32),
            pltpu.VMEM((2, chunks, half, CHUNK), BF16),
            pltpu.VMEM((2, chunks, half, CHUNK), BF16),
            pltpu.VMEM((chunks, half, CHUNK), BF16),
            pltpu.VMEM((2, main, wide), BF16),
            pltpu.VMEM((2, main, wide), BF16),
            dma((5,)), dma((2,)), dma((2,)), dma((2,)),
            dma((2, chips)), dma((2, chips)),
            dma((2, chips)), dma((2, chips)),
            dma((2, chunks)), dma((2, chunks)),
            dma((2, chips)), dma((2, chips)), dma((2,)),
            pltpu.SemaphoreType.REGULAR((2,)), pltpu.SemaphoreType.REGULAR((2,)),
        ],
        compiler_params=pltpu.CompilerParams(
            collective_id=0, has_side_effects=True, vmem_limit_bytes=40 << 20
        ),
    )(
        *[pltpu.with_memory_space_constraint(given, pltpu.HBM) for given in (
            routes_fwd.reshape(1, tokens), routes_bwd.reshape(1, tokens),
            sent_fwd[0], sent_bwd[0], router_w[0].T, w_up[0], w_down[0],
        )]
    )
    out_fwd, out_bwd = pl.pallas_call(
        write_kernel,
        out_shape=(shape, shape),
        in_specs=[vmem, vmem],
        out_specs=(hbm, hbm),
        scratch_shapes=[dma((2,))],
        compiler_params=pltpu.CompilerParams(has_side_effects=True, vmem_limit_bytes=8 << 20),
    )(out_fwd, out_bwd)
    return out_fwd[None], out_bwd[None]


def solution(mesh):
    return jax.shard_map(
        on_device,
        mesh=mesh,
        in_specs=(
            P("section", "expert", None),
            P("section", "expert", None),
            P("section", None, None),
            P("section", None, "expert"),
            P("section", "expert", None),
            P("section", "expert", None),
            P("section", "expert", None),
        ),
        out_specs=(P("section", "expert", None), P("section", "expert", None)),
        check_vma=False,
    )
```

```python
import functools

import jax
import jax.numpy as jnp
from jax import lax
from jax.experimental import pallas as pl
from jax.experimental.pallas import tpu as pltpu
from jax.sharding import PartitionSpec as P

MESH = pl.DeviceIdType.MESH
F32 = jnp.float32
BF16 = jnp.bfloat16
NT = (((1,), (1,)), ((), ()))
BASE = 16
BLOCK = 256
CHUNK = 512


def iota(shape, dim):
    return lax.broadcasted_iota(jnp.int32, shape, dim)


def ones_where(mask):
    return jnp.where(mask, 1.0, 0.0).astype(BF16)


def exact(a, b):
    return jnp.dot(a, b, preferred_element_type=F32).astype(BF16)


def to_blocks(rows, number):
    height = rows[0].shape[0]
    i, j = iota((number * 16, len(rows) * height), 0), iota((number * 16, len(rows) * height), 1)
    take = ones_where(j == (i % 16) * height + i // 16)
    return exact(take, jnp.concatenate(rows, axis=0))


def from_blocks(blocks, number, height):
    n = blocks.shape[0]
    i, j = iota((number * height, n), 0), iota((number * height, n), 1)
    take = ones_where(i == (j % 16) * height + j // 16)
    rows = exact(take, blocks)
    return [rows[q * height:(q + 1) * height] for q in range(number)]


def positions(chosen, experts):
    tokens = chosen.shape[1]
    named = iota((16, tokens), 0) == chosen
    earlier = ones_where(iota((tokens, tokens), 0) < iota((tokens, tokens), 1))
    counted = jnp.dot(ones_where(named), earlier, preferred_element_type=F32)
    place = jnp.sum(jnp.where(named, counted, 0.0), axis=0, keepdims=True)
    return place.astype(jnp.int32)


def slots(chosen, experts):
    place = positions(chosen, experts)
    return jnp.where(place < BASE, chosen * BASE + place, experts * BASE + chosen)


def layer_kernel(
    dims,
    rf_hbm, rb_hbm, fwd_hbm, bwd_hbm, router_hbm, up_hbm, down_hbm,
    out_ref,
    x_ref, rows_ref, pack_ref, up_ref, down_ref, hid_ref, router_ref, routes_ref, slot_ref, next_slots,
    part_out, part_in, own_part, y_ref, ret_ref,
    load_s, w_s, small_s, small_r, disp_s, disp_r, pair_s, pair_r, part_s, part_r, ret_s, ret_r, loc_s, chain, far, hop,
):
    chips, per_expert, experts, sections, tokens, width, hidden = dims
    blocks = width // BLOCK
    chunks = width // CHUNK
    main = chips * BASE
    spare = -(-chips // 16) * 16
    half = main + spare
    section = lax.axis_index("section")
    me = lax.axis_index("expert")
    core = lax.rem(me, 2)
    chip = me // 2
    sib = {"section": section, "expert": chip * 2 + 1 - core}
    odd = lax.rem(section, 2)
    there = (section + 1 - 2 * odd, lax.rem(section + sections - 1 + 2 * odd, sections))
    informer = lax.rem(section + sections - 2 + 4 * odd, sections)
    informed = lax.rem(section + sections + 2 - 4 * odd, sections)

    def partner(v):
        other, bit = chip, 1
        while bit <= v:
            if (v // bit) % 2:
                other = other + bit - 2 * bit * lax.rem(chip // bit, 2)
            bit *= 2
        return other

    def beside(v):
        return (partner(v) == chip + 1) | (partner(v) == chip - 1)

    order = [v for v in range(chips // 2, chips)] + [v for v in range(1, chips // 2)] + [0]

    def remote(src, dst, send, recv, device):
        return pltpu.make_async_remote_copy(
            src_ref=src, dst_ref=dst, send_sem=send, recv_sem=recv,
            device_id=device, device_id_type=MESH,
        )

    def arrived(dst, send, recv):
        remote(dst, dst, send, recv, sib).wait_recv()

    above = {"section": section, "expert": me + 2}
    below = {"section": section, "expert": me - 2}

    def signal(semaphore, device):
        pl.semaphore_signal(semaphore, inc=1, device_id=device, device_id_type=MESH)

    barrier = pltpu.get_barrier_semaphore()
    signal(barrier, {"section": there[0], "expert": me})
    signal(barrier, {"section": informer, "expert": me})
    signal(barrier, sib)

    @pl.when(chip > 0)
    def _():
        signal(barrier, below)

    @pl.when(chip < chips - 1)
    def _():
        signal(barrier, above)

    def loads_of(flip):
        routes, sent = (rb_hbm, rf_hbm), (fwd_hbm, bwd_hbm)
        return [
            pltpu.make_async_copy(routes[flip], routes_ref.at[0], load_s.at[0]),
            pltpu.make_async_copy(routes[1 - flip], routes_ref.at[1], load_s.at[1]),
            pltpu.make_async_copy(sent[flip], x_ref.at[0], load_s.at[2]),
            pltpu.make_async_copy(sent[1 - flip], x_ref.at[1], load_s.at[3]),
        ]

    for flip in range(2):
        @pl.when(odd == flip)
        def _():
            for load in loads_of(flip):
                load.start()

    loads = loads_of(0) + [pltpu.make_async_copy(router_hbm, router_ref, load_s.at[4])]
    loads[4].start()
    w_up_copy = pltpu.make_async_copy(up_hbm, up_ref, w_s.at[0])
    w_down_copy = pltpu.make_async_copy(down_hbm, down_ref, w_s.at[1])
    for m in range(2):
        loads[m].wait()
        slot_ref[m] = slots(routes_ref[m], experts)
    pl.semaphore_wait(barrier, 3 + jnp.where(chip > 0, 1, 0) + jnp.where(chip < chips - 1, 1, 0))

    sends = []

    def send(*args):
        copy = remote(*args)
        copy.start()
        sends.append(copy)

    def send_slots(m):
        send(slot_ref.at[m], next_slots.at[m], small_s.at[m], small_r.at[m], {"section": there[m], "expert": me})

    send_slots(0)
    signal(hop.at[0], {"section": informed, "expert": me})

    @pl.when(chip == 1)
    def _():
        signal(chain.at[0], above)

    @pl.when(chip == chips - 2)
    def _():
        signal(chain.at[1], below)

    def finish_chain():
        @pl.when(chip >= 2)
        def _():
            pl.semaphore_wait(chain.at[0], 1)

        @pl.when((chip >= 2) & (chip <= chips - 2))
        def _():
            signal(chain.at[0], above)

        @pl.when(chip <= chips - 3)
        def _():
            pl.semaphore_wait(chain.at[1], 1)

        @pl.when((chip >= 1) & (chip <= chips - 3))
        def _():
            signal(chain.at[1], below)

        signal(far.at[0], {"section": there[0], "expert": me})
        pl.semaphore_wait(hop.at[0], 1)
        send_slots(1)
        signal(far.at[1], {"section": there[1], "expert": me})

    for m in range(2):
        loads[2 + m].wait()
        arrived(next_slots.at[m], small_s.at[m], small_r.at[m])
        take = ones_where(iota((experts * BASE + 16, tokens), 0) == next_slots[m])
        extra = []
        for k in range(chunks):
            packed = exact(take, x_ref[m, :, k * CHUNK:(k + 1) * CHUNK])
            pack_ref[m, :, k * CHUNK:(k + 1) * CHUNK] = packed[0:experts * BASE]
            for b in range(CHUNK // BLOCK):
                extra.append(packed[experts * BASE:, b * BLOCK:(b + 1) * BLOCK])
        pack_ref[m, :, width:] = to_blocks(extra, experts)
        copies = {}
        for v in order:
            other = partner(v)
            copies[v] = remote(
                pack_ref.at[m, pl.ds(pl.multiple_of(other // per_expert * BASE, BASE), BASE), :],
                rows_ref.at[m, pl.ds(v * BASE, BASE), :],
                disp_s.at[m, v], disp_r.at[m, v],
                {"section": there[m], "expert": other * 2 + core},
            )
            sends.append(copies[v])
        if m == 0:
            for v in order:
                if v in (0, 1):
                    copies[v].start()
                elif v & (v + 1) == 0:
                    pl.when(beside(v))(copies[v].start)
            finish_chain()
            w_up_copy.start()
            w_down_copy.start()
        pl.semaphore_wait(far.at[m], 1)
        for v in order:
            if m == 1 or v & (v + 1):
                copies[v].start()
            elif v > 1:
                pl.when(jnp.logical_not(beside(v)))(copies[v].start)

    loads[4].wait()
    expert = chip // per_expert
    column = jnp.where(iota((experts, width), 0) == expert, router_ref[...], 0.0)
    column = jnp.sum(column, axis=0, keepdims=True)
    w_up_copy.wait()
    w_down_copy.wait()

    eye = ones_where(iota((tokens, tokens), 0) == iota((tokens, tokens), 1))
    unpack = []
    for m in range(2):
        slot = slot_ref[m]
        picks = [ones_where(iota((BASE, tokens), 0) == slot - d // per_expert * BASE) for d in range(chips)]
        row = iota((spare, tokens), 0)
        picks.append(ones_where((row // per_expert == slot - experts * BASE) & (row < chips)))
        unpack.append(
            lax.dot_general(eye, jnp.concatenate(picks, axis=0), NT, preferred_element_type=F32).astype(BF16)
        )

    for m in range(2):
        for v in order:
            mine = rows_ref.at[m, pl.ds(v * BASE, BASE), :]
            arrived(mine, disp_s.at[m, v], disp_r.at[m, v])
            send(mine, rows_ref.at[m, pl.ds(half + v * BASE, BASE), :], pair_s.at[m, v], pair_r.at[m, v], sib)

        def spread(start):
            found = from_blocks(rows_ref[m, start:start + main, width:], blocks, spare)
            for q in range(blocks):
                rows_ref[m, start + main:start + half, q * BLOCK:(q + 1) * BLOCK] = found[q]

        spread(0)
        total = jnp.zeros((half, 128), F32)
        for b in range(width // 128):
            cols = slice(b * 128, (b + 1) * 128)
            total += rows_ref[m, 0:half, cols].astype(F32) * column[:, cols]
        score = jax.nn.sigmoid(jnp.sum(total, axis=1, keepdims=True))
        first = lax.rem(chip, per_expert) == 0

        for v in order:
            arrived(rows_ref.at[m, pl.ds(half + v * BASE, BASE), :], pair_s.at[m, v], pair_r.at[m, v])
        spread(half)
        hid_ref[m] = jax.nn.silu(
            jnp.dot(rows_ref[m, :, 0:width], up_ref[...], preferred_element_type=F32)
        ).astype(BF16)

        for k in range(chunks):
            part = exact(hid_ref[m], down_ref[:, k * CHUNK:(k + 1) * CHUNK])
            part_out[m, k] = part[half:]
            own_part[k] = part[0:half]
            send(part_out.at[m, k], part_in.at[m, k], part_s.at[m, k], part_r.at[m, k], sib)
        extra = []
        for k in range(chunks):
            arrived(part_in.at[m, k], part_s.at[m, k], part_r.at[m, k])
            added = score * (own_part[k].astype(F32) + part_in[m, k].astype(F32))
            x = rows_ref[m, 0:half, k * CHUNK:(k + 1) * CHUNK].astype(F32)
            if per_expert > 1:
                x = jnp.where(first, x, 0.0)
            y = (x + added).astype(BF16)
            y_ref[m, :, k * CHUNK:(k + 1) * CHUNK] = y[0:main]
            for b in range(CHUNK // BLOCK):
                extra.append(y[main:, b * BLOCK:(b + 1) * BLOCK])
        y_ref[m, :, width:] = to_blocks(extra, chips)
        for v in order:
            y = y_ref.at[m, pl.ds(v * BASE, BASE), :]
            home = ret_ref.at[m, pl.ds(pl.multiple_of(chip * BASE, BASE), BASE), :]
            if v == 0:
                local = pltpu.make_async_copy(y, home, loc_s.at[m])
                local.start()
            else:
                send(y, home, ret_s.at[m, v], ret_r.at[m, v], {"section": section, "expert": partner(v) * 2 + core})

    for m in range(2):
        for v in order:
            here = ret_ref.at[m, pl.ds(pl.multiple_of(partner(v) * BASE, BASE), BASE), :]
            if v == 0:
                pltpu.make_async_copy(here, here, loc_s.at[m]).wait()
            else:
                arrived(here, ret_s.at[m, v], ret_r.at[m, v])
        extra = from_blocks(ret_ref[m, :, width:], blocks, spare)
        for k in range(chunks):
            found = jnp.concatenate(extra[k * CHUNK // BLOCK:(k + 1) * CHUNK // BLOCK], axis=1)
            came = jnp.concatenate([ret_ref[m, :, k * CHUNK:(k + 1) * CHUNK], found], axis=0)
            out_ref[m, :, k * CHUNK:(k + 1) * CHUNK] = exact(unpack[m], came)

    for copy in sends:
        copy.wait_send()


def write_kernel(both, out_fwd, out_bwd, sems):
    odd = lax.rem(lax.axis_index("section"), 2)
    stores = [
        pltpu.make_async_copy(both.at[1 - odd], out_fwd, sems.at[0]),
        pltpu.make_async_copy(both.at[odd], out_bwd, sems.at[1]),
    ]
    for store in stores:
        store.start()
    for store in stores:
        store.wait()


def on_device(sent_fwd, sent_bwd, router_w, w_up, w_down, routes_fwd, routes_bwd):
    tokens, width = sent_fwd.shape[1:]
    hidden = w_up.shape[2]
    experts = router_w.shape[2]
    sections = lax.axis_size("section")
    chips = lax.axis_size("expert") // 2
    per_expert = chips // experts
    dims = (chips, per_expert, experts, sections, tokens, width, hidden)
    chunks = width // CHUNK
    wide = width + BLOCK
    main = chips * BASE
    half = main + -(-chips // 16) * 16
    dma = pltpu.SemaphoreType.DMA
    hbm = pl.BlockSpec(memory_space=pltpu.HBM)
    vmem = pl.BlockSpec(memory_space=pltpu.VMEM)
    shape = jax.ShapeDtypeStruct((tokens, width), BF16)
    assert sections % 2 == 0 and sections > 2
    both = pl.pallas_call(
        functools.partial(layer_kernel, dims),
        out_shape=jax.ShapeDtypeStruct((2, tokens, width), BF16),
        in_specs=[hbm] * 7,
        out_specs=vmem,
        scratch_shapes=[
            pltpu.VMEM((2, tokens, width), BF16),
            pltpu.VMEM((2, 2 * half, wide), BF16),
            pltpu.VMEM((2, experts * BASE, wide), BF16),
            pltpu.VMEM((width, hidden), BF16),
            pltpu.VMEM((hidden, width), BF16),
            pltpu.VMEM((2, 2 * half, hidden), BF16),
            pltpu.VMEM((experts, width), F32),
            pltpu.VMEM((2, 1, tokens), jnp.int32),
            pltpu.VMEM((2, 1, tokens), jnp.int32),
            pltpu.VMEM((2, 1, tokens), jnp.int32),
            pltpu.VMEM((2, chunks, half, CHUNK), BF16),
            pltpu.VMEM((2, chunks, half, CHUNK), BF16),
            pltpu.VMEM((chunks, half, CHUNK), BF16),
            pltpu.VMEM((2, main, wide), BF16),
            pltpu.VMEM((2, main, wide), BF16),
            dma((5,)), dma((2,)), dma((2,)), dma((2,)),
            dma((2, chips)), dma((2, chips)),
            dma((2, chips)), dma((2, chips)),
            dma((2, chunks)), dma((2, chunks)),
            dma((2, chips)), dma((2, chips)), dma((2,)),
            pltpu.SemaphoreType.REGULAR((2,)), pltpu.SemaphoreType.REGULAR((2,)), pltpu.SemaphoreType.REGULAR((1,)),
        ],
        compiler_params=pltpu.CompilerParams(
            collective_id=0, has_side_effects=True, vmem_limit_bytes=40 << 20
        ),
    )(
        *[pltpu.with_memory_space_constraint(given, pltpu.HBM) for given in (
            routes_fwd.reshape(1, tokens), routes_bwd.reshape(1, tokens),
            sent_fwd[0], sent_bwd[0], router_w[0].T, w_up[0], w_down[0],
        )]
    )
    out_fwd, out_bwd = pl.pallas_call(
        write_kernel,
        out_shape=(shape, shape),
        in_specs=[vmem],
        out_specs=(hbm, hbm),
        scratch_shapes=[dma((2,))],
        compiler_params=pltpu.CompilerParams(has_side_effects=True, vmem_limit_bytes=8 << 20),
    )(both)
    return out_fwd[None], out_bwd[None]


def solution(mesh):
    return jax.shard_map(
        on_device,
        mesh=mesh,
        in_specs=(
            P("section", "expert", None),
            P("section", "expert", None),
            P("section", None, None),
            P("section", None, "expert"),
            P("section", "expert", None),
            P("section", "expert", None),
            P("section", "expert", None),
        ),
        out_specs=(P("section", "expert", None), P("section", "expert", None)),
        check_vma=False,
    )
```

```python
import functools

import jax
import jax.numpy as jnp
from jax import lax
from jax.experimental import pallas as pl
from jax.experimental.pallas import tpu as pltpu
from jax.sharding import PartitionSpec as P

MESH = pl.DeviceIdType.MESH
F32 = jnp.float32
BF16 = jnp.bfloat16
NT = (((1,), (1,)), ((), ()))
BASE = 16
BLOCK = 256
CHUNK = 512


def iota(shape, dim):
    return lax.broadcasted_iota(jnp.int32, shape, dim)


def ones_where(mask):
    return jnp.where(mask, 1.0, 0.0).astype(BF16)


def exact(a, b):
    return jnp.dot(a, b, preferred_element_type=F32).astype(BF16)


def to_blocks(rows, number):
    height = rows[0].shape[0]
    i, j = iota((number * 16, len(rows) * height), 0), iota((number * 16, len(rows) * height), 1)
    take = ones_where(j == (i % 16) * height + i // 16)
    return exact(take, jnp.concatenate(rows, axis=0))


def from_blocks(blocks, number, height):
    n = blocks.shape[0]
    i, j = iota((number * height, n), 0), iota((number * height, n), 1)
    take = ones_where(i == (j % 16) * height + j // 16)
    rows = exact(take, blocks)
    return [rows[q * height:(q + 1) * height] for q in range(number)]


def positions(chosen, experts):
    tokens = chosen.shape[1]
    named = iota((16, tokens), 0) == chosen
    earlier = ones_where(iota((tokens, tokens), 0) < iota((tokens, tokens), 1))
    counted = jnp.dot(ones_where(named), earlier, preferred_element_type=F32)
    place = jnp.sum(jnp.where(named, counted, 0.0), axis=0, keepdims=True)
    return place.astype(jnp.int32)


def slots(chosen, experts):
    place = positions(chosen, experts)
    return jnp.where(place < BASE, chosen * BASE + place, experts * BASE + chosen)


def layer_kernel(
    dims,
    rf_hbm, rb_hbm, fwd_hbm, bwd_hbm, router_hbm, up_hbm, down_hbm,
    out_ref,
    x_ref, rows_ref, pack_ref, up_ref, down_ref, hid_ref, router_ref, routes_ref, slot_ref, next_slots,
    part_out, part_in, own_part, y_ref, ret_ref, whole_ref, split_ref,
    load_s, w_s, small_s, small_r, disp_s, disp_r, pair_s, pair_r, part_s, part_r, ret_s, ret_r, loc_s, chain, far, hop,
):
    chips, per_expert, experts, sections, tokens, width, hidden = dims
    blocks = width // BLOCK
    chunks = width // CHUNK
    main = chips * BASE
    spare = -(-chips // 16) * 16
    half = main + spare
    section = lax.axis_index("section")
    me = lax.axis_index("expert")
    core = lax.rem(me, 2)
    chip = me // 2
    sib = {"section": section, "expert": chip * 2 + 1 - core}
    odd = lax.rem(section, 2)
    there = (section + 1 - 2 * odd, lax.rem(section + sections - 1 + 2 * odd, sections))
    informer = lax.rem(section + sections - 2 + 4 * odd, sections)
    informed = lax.rem(section + sections + 2 - 4 * odd, sections)

    def partner(v):
        other, bit = chip, 1
        while bit <= v:
            if (v // bit) % 2:
                other = other + bit - 2 * bit * lax.rem(chip // bit, 2)
            bit *= 2
        return other

    def beside(v):
        return (partner(v) == chip + 1) | (partner(v) == chip - 1)

    order = [v for v in range(chips // 2, chips)] + [v for v in range(1, chips // 2)] + [0]

    def remote(src, dst, send, recv, device):
        return pltpu.make_async_remote_copy(
            src_ref=src, dst_ref=dst, send_sem=send, recv_sem=recv,
            device_id=device, device_id_type=MESH,
        )

    def arrived(dst, send, recv):
        remote(dst, dst, send, recv, sib).wait_recv()

    above = {"section": section, "expert": me + 2}
    below = {"section": section, "expert": me - 2}

    def signal(semaphore, device):
        pl.semaphore_signal(semaphore, inc=1, device_id=device, device_id_type=MESH)

    barrier = pltpu.get_barrier_semaphore()
    signal(barrier, {"section": there[0], "expert": me})
    signal(barrier, {"section": informer, "expert": me})
    signal(barrier, sib)

    @pl.when(chip > 0)
    def _():
        signal(barrier, below)

    @pl.when(chip < chips - 1)
    def _():
        signal(barrier, above)

    def loads_of(flip):
        routes, sent = (rb_hbm, rf_hbm), (fwd_hbm, bwd_hbm)
        return [
            pltpu.make_async_copy(routes[flip], routes_ref.at[0], load_s.at[0]),
            pltpu.make_async_copy(routes[1 - flip], routes_ref.at[1], load_s.at[1]),
            pltpu.make_async_copy(sent[flip], x_ref.at[0], load_s.at[2]),
            pltpu.make_async_copy(sent[1 - flip], x_ref.at[1], load_s.at[3]),
        ]

    for flip in range(2):
        @pl.when(odd == flip)
        def _():
            for load in loads_of(flip):
                load.start()

    loads = loads_of(0) + [pltpu.make_async_copy(router_hbm, router_ref, load_s.at[4])]
    loads[4].start()
    w_up_copy = pltpu.make_async_copy(up_hbm, up_ref, w_s.at[0])
    w_down_copy = pltpu.make_async_copy(down_hbm, down_ref, w_s.at[1])
    for m in range(2):
        loads[m].wait()
        slot_ref[m] = slots(routes_ref[m], experts)
    pl.semaphore_wait(barrier, 3 + jnp.where(chip > 0, 1, 0) + jnp.where(chip < chips - 1, 1, 0))

    sends = []

    backs = ([], [])

    def send(*args):
        copy = remote(*args)
        copy.start()
        sends.append(copy)

    def back(m, *args):
        copy = remote(*args)
        copy.start()
        backs[m].append(copy)

    def send_slots(m):
        send(slot_ref.at[m], next_slots.at[m], small_s.at[m], small_r.at[m], {"section": there[m], "expert": me})

    send_slots(0)
    signal(hop.at[0], {"section": informed, "expert": me})

    @pl.when(chip == 1)
    def _():
        signal(chain.at[0], above)

    @pl.when(chip == chips - 2)
    def _():
        signal(chain.at[1], below)

    def finish_chain():
        @pl.when(chip >= 2)
        def _():
            pl.semaphore_wait(chain.at[0], 1)

        @pl.when((chip >= 2) & (chip <= chips - 2))
        def _():
            signal(chain.at[0], above)

        @pl.when(chip <= chips - 3)
        def _():
            pl.semaphore_wait(chain.at[1], 1)

        @pl.when((chip >= 1) & (chip <= chips - 3))
        def _():
            signal(chain.at[1], below)

        signal(far.at[0], {"section": there[0], "expert": me})
        pl.semaphore_wait(hop.at[0], 1)
        send_slots(1)
        signal(far.at[1], {"section": there[1], "expert": me})

    for m in range(2):
        loads[2 + m].wait()
        arrived(next_slots.at[m], small_s.at[m], small_r.at[m])
        take = ones_where(iota((experts * BASE + 16, tokens), 0) == next_slots[m])
        extra = []
        for k in range(chunks):
            packed = exact(take, x_ref[m, :, k * CHUNK:(k + 1) * CHUNK])
            pack_ref[m, :, k * CHUNK:(k + 1) * CHUNK] = packed[0:experts * BASE]
            for b in range(CHUNK // BLOCK):
                extra.append(packed[experts * BASE:, b * BLOCK:(b + 1) * BLOCK])
        pack_ref[m, :, width:] = to_blocks(extra, experts)
        copies = {}
        for v in order:
            other = partner(v)
            copies[v] = remote(
                pack_ref.at[m, pl.ds(pl.multiple_of(other // per_expert * BASE, BASE), BASE), :],
                rows_ref.at[m, pl.ds(v * BASE, BASE), :],
                disp_s.at[m, v], disp_r.at[m, v],
                {"section": there[m], "expert": other * 2 + core},
            )
            sends.append(copies[v])
        for v in order:
            if m == 0 and v > 1 and v & (v + 1) == 0:
                pl.when(beside(v))(copies[v].start)
        if m == 0:
            finish_chain()
            w_up_copy.start()
            w_down_copy.start()
        pl.semaphore_wait(far.at[m], 1)
        for v in order:
            if m == 0 and v > 1 and v & (v + 1) == 0:
                pl.when(jnp.logical_not(beside(v)))(copies[v].start)
            else:
                copies[v].start()

    loads[4].wait()
    expert = chip // per_expert
    column = jnp.where(iota((experts, width), 0) == expert, router_ref[...], 0.0)
    column = jnp.sum(column, axis=0, keepdims=True)
    w_up_copy.wait()
    w_down_copy.wait()

    eye = ones_where(iota((tokens, tokens), 0) == iota((tokens, tokens), 1))
    lane = iota((tokens, main), 1)
    within, expert_of = lane % BASE, lane // (BASE * per_expert)
    for m in range(2):
        slot = jnp.broadcast_to(slot_ref[m].astype(F32), (8, tokens)).astype(BF16)
        slot = lax.dot_general(eye, slot, NT, preferred_element_type=F32)[:, 0:1].astype(jnp.int32)
        whole_ref[m] = ones_where(expert_of * BASE + within == slot)
        split = expert_of + experts * BASE == slot
        for q in range(blocks):
            split_ref[m, q] = ones_where(split & (within == q))

    for m in range(2):
        for v in order:
            mine = rows_ref.at[m, pl.ds(v * BASE, BASE), :]
            arrived(mine, disp_s.at[m, v], disp_r.at[m, v])
            send(mine, rows_ref.at[m, pl.ds(half + v * BASE, BASE), :], pair_s.at[m, v], pair_r.at[m, v], sib)

        def spread(start):
            found = from_blocks(rows_ref[m, start:start + main, width:], blocks, spare)
            for q in range(blocks):
                rows_ref[m, start + main:start + half, q * BLOCK:(q + 1) * BLOCK] = found[q]

        spread(0)
        total = jnp.zeros((half, 128), F32)
        for b in range(width // 128):
            cols = slice(b * 128, (b + 1) * 128)
            total += rows_ref[m, 0:half, cols].astype(F32) * column[:, cols]
        score = jax.nn.sigmoid(jnp.sum(total, axis=1, keepdims=True))
        first = lax.rem(chip, per_expert) == 0

        for v in order:
            arrived(rows_ref.at[m, pl.ds(half + v * BASE, BASE), :], pair_s.at[m, v], pair_r.at[m, v])
        spread(half)
        hid_ref[m] = jax.nn.silu(
            jnp.dot(rows_ref[m, :, 0:width], up_ref[...], preferred_element_type=F32)
        ).astype(BF16)

        for k in range(chunks):
            part = exact(hid_ref[m], down_ref[:, k * CHUNK:(k + 1) * CHUNK])
            part_out[m, k] = part[half:]
            own_part[k] = part[0:half]
            send(part_out.at[m, k], part_in.at[m, k], part_s.at[m, k], part_r.at[m, k], sib)
        extra = []
        for k in range(chunks):
            arrived(part_in.at[m, k], part_s.at[m, k], part_r.at[m, k])
            added = score * (own_part[k].astype(F32) + part_in[m, k].astype(F32))
            x = rows_ref[m, 0:half, k * CHUNK:(k + 1) * CHUNK].astype(F32)
            if per_expert > 1:
                x = jnp.where(first, x, 0.0)
            y = (x + added).astype(BF16)
            y_ref[m, :, k * CHUNK:(k + 1) * CHUNK] = y[0:main]
            for b in range(CHUNK // BLOCK):
                extra.append(y[main:, b * BLOCK:(b + 1) * BLOCK])
        y_ref[m, :, width:] = to_blocks(extra, chips)
        for v in order:
            y = y_ref.at[m, pl.ds(v * BASE, BASE), :]
            home = ret_ref.at[m, pl.ds(pl.multiple_of(chip * BASE, BASE), BASE), :]
            if v == 0:
                pltpu.make_async_copy(y, home, loc_s.at[m]).start()
            else:
                back(m, y, home, ret_s.at[m, v], ret_r.at[m, v], {"section": section, "expert": partner(v) * 2 + core})

    for copy in sends:
        copy.wait_send()
    for m in range(2):
        for v in order:
            here = ret_ref.at[m, pl.ds(pl.multiple_of(partner(v) * BASE, BASE), BASE), :]
            if v == 0:
                pltpu.make_async_copy(here, here, loc_s.at[m]).wait()
            else:
                arrived(here, ret_s.at[m, v], ret_r.at[m, v])
        for q in range(blocks):
            cols = slice(q * BLOCK, (q + 1) * BLOCK)
            found = jnp.dot(whole_ref[m], ret_ref[m, :, cols], preferred_element_type=F32)
            found += jnp.dot(split_ref[m, q], ret_ref[m, :, width:], preferred_element_type=F32)
            out_ref[m, :, cols] = found.astype(BF16)
        for copy in backs[m]:
            copy.wait_send()


def write_kernel(both, out_fwd, out_bwd, sems):
    odd = lax.rem(lax.axis_index("section"), 2)
    stores = [
        pltpu.make_async_copy(both.at[1 - odd], out_fwd, sems.at[0]),
        pltpu.make_async_copy(both.at[odd], out_bwd, sems.at[1]),
    ]
    for store in stores:
        store.start()
    for store in stores:
        store.wait()


def on_device(sent_fwd, sent_bwd, router_w, w_up, w_down, routes_fwd, routes_bwd):
    tokens, width = sent_fwd.shape[1:]
    hidden = w_up.shape[2]
    experts = router_w.shape[2]
    sections = lax.axis_size("section")
    chips = lax.axis_size("expert") // 2
    per_expert = chips // experts
    dims = (chips, per_expert, experts, sections, tokens, width, hidden)
    chunks = width // CHUNK
    wide = width + BLOCK
    main = chips * BASE
    half = main + -(-chips // 16) * 16
    dma = pltpu.SemaphoreType.DMA
    hbm = pl.BlockSpec(memory_space=pltpu.HBM)
    vmem = pl.BlockSpec(memory_space=pltpu.VMEM)
    shape = jax.ShapeDtypeStruct((tokens, width), BF16)
    assert sections % 2 == 0 and sections > 2
    both = pl.pallas_call(
        functools.partial(layer_kernel, dims),
        out_shape=jax.ShapeDtypeStruct((2, tokens, width), BF16),
        in_specs=[hbm] * 7,
        out_specs=vmem,
        scratch_shapes=[
            pltpu.VMEM((2, tokens, width), BF16),
            pltpu.VMEM((2, 2 * half, wide), BF16),
            pltpu.VMEM((2, experts * BASE, wide), BF16),
            pltpu.VMEM((width, hidden), BF16),
            pltpu.VMEM((hidden, width), BF16),
            pltpu.VMEM((2, 2 * half, hidden), BF16),
            pltpu.VMEM((experts, width), F32),
            pltpu.VMEM((2, 1, tokens), jnp.int32),
            pltpu.VMEM((2, 1, tokens), jnp.int32),
            pltpu.VMEM((2, 1, tokens), jnp.int32),
            pltpu.VMEM((2, chunks, half, CHUNK), BF16),
            pltpu.VMEM((2, chunks, half, CHUNK), BF16),
            pltpu.VMEM((chunks, half, CHUNK), BF16),
            pltpu.VMEM((2, main, wide), BF16),
            pltpu.VMEM((2, main, wide), BF16),
            pltpu.VMEM((2, tokens, main), BF16),
            pltpu.VMEM((2, width // BLOCK, tokens, main), BF16),
            dma((5,)), dma((2,)), dma((2,)), dma((2,)),
            dma((2, chips)), dma((2, chips)),
            dma((2, chips)), dma((2, chips)),
            dma((2, chunks)), dma((2, chunks)),
            dma((2, chips)), dma((2, chips)), dma((2,)),
            pltpu.SemaphoreType.REGULAR((2,)), pltpu.SemaphoreType.REGULAR((2,)), pltpu.SemaphoreType.REGULAR((1,)),
        ],
        compiler_params=pltpu.CompilerParams(
            collective_id=0, has_side_effects=True, vmem_limit_bytes=40 << 20
        ),
    )(
        *[pltpu.with_memory_space_constraint(given, pltpu.HBM) for given in (
            routes_fwd.reshape(1, tokens), routes_bwd.reshape(1, tokens),
            sent_fwd[0], sent_bwd[0], router_w[0].T, w_up[0], w_down[0],
        )]
    )
    out_fwd, out_bwd = pl.pallas_call(
        write_kernel,
        out_shape=(shape, shape),
        in_specs=[vmem],
        out_specs=(hbm, hbm),
        scratch_shapes=[dma((2,))],
        compiler_params=pltpu.CompilerParams(has_side_effects=True, vmem_limit_bytes=8 << 20),
    )(both)
    return out_fwd[None], out_bwd[None]


def solution(mesh):
    return jax.shard_map(
        on_device,
        mesh=mesh,
        in_specs=(
            P("section", "expert", None),
            P("section", "expert", None),
            P("section", None, None),
            P("section", None, "expert"),
            P("section", "expert", None),
            P("section", "expert", None),
            P("section", "expert", None),
        ),
        out_specs=(P("section", "expert", None), P("section", "expert", None)),
        check_vma=False,
    )
```

```python
import functools

import jax
import jax.numpy as jnp
from jax import lax
from jax.experimental import pallas as pl
from jax.experimental.pallas import tpu as pltpu
from jax.sharding import PartitionSpec as P

MESH = pl.DeviceIdType.MESH
F32 = jnp.float32
BF16 = jnp.bfloat16
NT = (((1,), (1,)), ((), ()))
BASE = 16
BLOCK = 256
CHUNK = 512


def iota(shape, dim):
    return lax.broadcasted_iota(jnp.int32, shape, dim)


def ones_where(mask):
    return jnp.where(mask, 1.0, 0.0).astype(BF16)


def exact(a, b):
    return jnp.dot(a, b, preferred_element_type=F32).astype(BF16)


def to_blocks(rows, number):
    height = rows[0].shape[0]
    i, j = iota((number * 16, len(rows) * height), 0), iota((number * 16, len(rows) * height), 1)
    take = ones_where(j == (i % 16) * height + i // 16)
    return exact(take, jnp.concatenate(rows, axis=0))


def from_blocks(blocks, number, height):
    n = blocks.shape[0]
    i, j = iota((number * height, n), 0), iota((number * height, n), 1)
    take = ones_where(i == (j % 16) * height + j // 16)
    rows = exact(take, blocks)
    return [rows[q * height:(q + 1) * height] for q in range(number)]


def positions(chosen, experts):
    tokens = chosen.shape[1]
    named = iota((16, tokens), 0) == chosen
    earlier = ones_where(iota((tokens, tokens), 0) < iota((tokens, tokens), 1))
    counted = jnp.dot(ones_where(named), earlier, preferred_element_type=F32)
    place = jnp.sum(jnp.where(named, counted, 0.0), axis=0, keepdims=True)
    return place.astype(jnp.int32)


def slots(chosen, experts):
    place = positions(chosen, experts)
    return jnp.where(place < BASE, chosen * BASE + place, experts * BASE + chosen)


def layer_kernel(
    dims,
    rf_hbm, rb_hbm, fwd_hbm, bwd_hbm, router_hbm, up_hbm, down_hbm,
    out_ref,
    x_ref, rows_ref, pack_ref, up_ref, down_ref, hid_ref, router_ref, routes_ref, slot_ref, next_slots,
    part_out, part_in, own_part, y_ref, ret_ref, whole_ref, split_ref,
    load_s, w_s, small_s, small_r, disp_s, disp_r, pair_s, pair_r, part_s, part_r, ret_s, ret_r, loc_s, chain, far, hop,
):
    chips, per_expert, experts, sections, tokens, width, hidden = dims
    blocks = width // BLOCK
    chunks = width // CHUNK
    main = chips * BASE
    spare = -(-chips // 16) * 16
    half = main + spare
    section = lax.axis_index("section")
    me = lax.axis_index("expert")
    core = lax.rem(me, 2)
    chip = me // 2
    sib = {"section": section, "expert": chip * 2 + 1 - core}
    odd = lax.rem(section, 2)
    there = (section + 1 - 2 * odd, lax.rem(section + sections - 1 + 2 * odd, sections))
    informer = lax.rem(section + sections - 2 + 4 * odd, sections)
    informed = lax.rem(section + sections + 2 - 4 * odd, sections)

    def partner(v):
        other, bit = chip, 1
        while bit <= v:
            if (v // bit) % 2:
                other = other + bit - 2 * bit * lax.rem(chip // bit, 2)
            bit *= 2
        return other

    def beside(v):
        return (partner(v) == chip + 1) | (partner(v) == chip - 1)

    order = [v for v in range(chips // 2, chips)] + [v for v in range(1, chips // 2)] + [0]

    def remote(src, dst, send, recv, device):
        return pltpu.make_async_remote_copy(
            src_ref=src, dst_ref=dst, send_sem=send, recv_sem=recv,
            device_id=device, device_id_type=MESH,
        )

    def arrived(dst, send, recv):
        remote(dst, dst, send, recv, sib).wait_recv()

    above = {"section": section, "expert": me + 2}
    below = {"section": section, "expert": me - 2}

    def signal(semaphore, device):
        pl.semaphore_signal(semaphore, inc=1, device_id=device, device_id_type=MESH)

    barrier = pltpu.get_barrier_semaphore()
    signal(barrier, {"section": there[0], "expert": me})
    signal(barrier, {"section": informer, "expert": me})
    signal(barrier, sib)

    @pl.when(chip > 0)
    def _():
        signal(barrier, below)

    @pl.when(chip < chips - 1)
    def _():
        signal(barrier, above)

    def loads_of(flip):
        routes, sent = (rb_hbm, rf_hbm), (fwd_hbm, bwd_hbm)
        return [
            pltpu.make_async_copy(routes[flip], routes_ref.at[0], load_s.at[0]),
            pltpu.make_async_copy(routes[1 - flip], routes_ref.at[1], load_s.at[1]),
            pltpu.make_async_copy(sent[flip], x_ref.at[0], load_s.at[2]),
            pltpu.make_async_copy(sent[1 - flip], x_ref.at[1], load_s.at[3]),
        ]

    for flip in range(2):
        @pl.when(odd == flip)
        def _():
            for load in loads_of(flip):
                load.start()

    loads = loads_of(0) + [pltpu.make_async_copy(router_hbm, router_ref, load_s.at[4])]
    loads[4].start()
    w_up_copy = pltpu.make_async_copy(up_hbm, up_ref, w_s.at[0])
    w_down_copy = pltpu.make_async_copy(down_hbm, down_ref, w_s.at[1])
    for m in range(2):
        loads[m].wait()
        slot_ref[m] = slots(routes_ref[m], experts)
    pl.semaphore_wait(barrier, 3 + jnp.where(chip > 0, 1, 0) + jnp.where(chip < chips - 1, 1, 0))

    sends = []

    backs = ([], [])

    def send(*args):
        copy = remote(*args)
        copy.start()
        sends.append(copy)

    def back(m, *args):
        copy = remote(*args)
        copy.start()
        backs[m].append(copy)

    def send_slots(m):
        send(slot_ref.at[m], next_slots.at[m], small_s.at[m], small_r.at[m], {"section": there[m], "expert": me})

    send_slots(0)
    signal(hop.at[0], {"section": informed, "expert": me})

    @pl.when(chip == 1)
    def _():
        signal(chain.at[0], above)

    @pl.when(chip == chips - 2)
    def _():
        signal(chain.at[1], below)

    def finish_chain():
        @pl.when(chip >= 2)
        def _():
            pl.semaphore_wait(chain.at[0], 1)

        @pl.when((chip >= 2) & (chip <= chips - 2))
        def _():
            signal(chain.at[0], above)

        @pl.when(chip <= chips - 3)
        def _():
            pl.semaphore_wait(chain.at[1], 1)

        @pl.when((chip >= 1) & (chip <= chips - 3))
        def _():
            signal(chain.at[1], below)

        signal(far.at[0], {"section": there[0], "expert": me})
        signal(far.at[1], {"section": there[1], "expert": me})

    for m in range(2):
        loads[2 + m].wait()
        arrived(next_slots.at[m], small_s.at[m], small_r.at[m])
        take = ones_where(iota((experts * BASE + 16, tokens), 0) == next_slots[m])
        extra = []
        for k in range(chunks):
            packed = exact(take, x_ref[m, :, k * CHUNK:(k + 1) * CHUNK])
            pack_ref[m, :, k * CHUNK:(k + 1) * CHUNK] = packed[0:experts * BASE]
            for b in range(CHUNK // BLOCK):
                extra.append(packed[experts * BASE:, b * BLOCK:(b + 1) * BLOCK])
        pack_ref[m, :, width:] = to_blocks(extra, experts)
        copies = {}
        for v in order:
            other = partner(v)
            copies[v] = remote(
                pack_ref.at[m, pl.ds(pl.multiple_of(other // per_expert * BASE, BASE), BASE), :],
                rows_ref.at[m, pl.ds(v * BASE, BASE), :],
                disp_s.at[m, v], disp_r.at[m, v],
                {"section": there[m], "expert": other * 2 + core},
            )
            sends.append(copies[v])
        if m == 0:
            pl.semaphore_wait(hop.at[0], 1)
            send_slots(1)
        for v in order:
            if m == 0 and v > 1 and v & (v + 1) == 0:
                pl.when(beside(v))(copies[v].start)
        if m == 0:
            finish_chain()
            w_up_copy.start()
            w_down_copy.start()
        pl.semaphore_wait(far.at[m], 1)
        for v in order:
            if m == 0 and v > 1 and v & (v + 1) == 0:
                pl.when(jnp.logical_not(beside(v)))(copies[v].start)
            else:
                copies[v].start()

    loads[4].wait()
    expert = chip // per_expert
    column = jnp.where(iota((experts, width), 0) == expert, router_ref[...], 0.0)
    column = jnp.sum(column, axis=0, keepdims=True)
    w_up_copy.wait()
    w_down_copy.wait()

    eye = ones_where(iota((tokens, tokens), 0) == iota((tokens, tokens), 1))
    lane = iota((tokens, main), 1)
    within, expert_of = lane % BASE, lane // (BASE * per_expert)
    for m in range(2):
        slot = jnp.broadcast_to(slot_ref[m].astype(F32), (8, tokens)).astype(BF16)
        slot = lax.dot_general(eye, slot, NT, preferred_element_type=F32)[:, 0:1].astype(jnp.int32)
        whole_ref[m] = ones_where(expert_of * BASE + within == slot)
        split = expert_of + experts * BASE == slot
        for q in range(blocks):
            split_ref[m, q] = ones_where(split & (within == q))

    for m in range(2):
        for v in order:
            mine = rows_ref.at[m, pl.ds(v * BASE, BASE), :]
            arrived(mine, disp_s.at[m, v], disp_r.at[m, v])
            send(mine, rows_ref.at[m, pl.ds(half + v * BASE, BASE), :], pair_s.at[m, v], pair_r.at[m, v], sib)

        def spread(start):
            found = from_blocks(rows_ref[m, start:start + main, width:], blocks, spare)
            for q in range(blocks):
                rows_ref[m, start + main:start + half, q * BLOCK:(q + 1) * BLOCK] = found[q]

        spread(0)
        total = jnp.zeros((half, 128), F32)
        for b in range(width // 128):
            cols = slice(b * 128, (b + 1) * 128)
            total += rows_ref[m, 0:half, cols].astype(F32) * column[:, cols]
        score = jax.nn.sigmoid(jnp.sum(total, axis=1, keepdims=True))
        first = lax.rem(chip, per_expert) == 0

        for v in order:
            arrived(rows_ref.at[m, pl.ds(half + v * BASE, BASE), :], pair_s.at[m, v], pair_r.at[m, v])
        spread(half)
        hid_ref[m] = jax.nn.silu(
            jnp.dot(rows_ref[m, :, 0:width], up_ref[...], preferred_element_type=F32)
        ).astype(BF16)

        for k in range(chunks):
            part = exact(hid_ref[m], down_ref[:, k * CHUNK:(k + 1) * CHUNK])
            part_out[m, k] = part[half:]
            own_part[k] = part[0:half]
            send(part_out.at[m, k], part_in.at[m, k], part_s.at[m, k], part_r.at[m, k], sib)
        extra = []
        for k in range(chunks):
            arrived(part_in.at[m, k], part_s.at[m, k], part_r.at[m, k])
            added = score * (own_part[k].astype(F32) + part_in[m, k].astype(F32))
            x = rows_ref[m, 0:half, k * CHUNK:(k + 1) * CHUNK].astype(F32)
            if per_expert > 1:
                x = jnp.where(first, x, 0.0)
            y = (x + added).astype(BF16)
            y_ref[m, :, k * CHUNK:(k + 1) * CHUNK] = y[0:main]
            for b in range(CHUNK // BLOCK):
                extra.append(y[main:, b * BLOCK:(b + 1) * BLOCK])
        y_ref[m, :, width:] = to_blocks(extra, chips)
        for v in order:
            y = y_ref.at[m, pl.ds(v * BASE, BASE), :]
            home = ret_ref.at[m, pl.ds(pl.multiple_of(chip * BASE, BASE), BASE), :]
            if v == 0:
                pltpu.make_async_copy(y, home, loc_s.at[m]).start()
            else:
                back(m, y, home, ret_s.at[m, v], ret_r.at[m, v], {"section": section, "expert": partner(v) * 2 + core})

    for copy in sends:
        copy.wait_send()
    for m in range(2):
        for v in order:
            here = ret_ref.at[m, pl.ds(pl.multiple_of(partner(v) * BASE, BASE), BASE), :]
            if v == 0:
                pltpu.make_async_copy(here, here, loc_s.at[m]).wait()
            else:
                arrived(here, ret_s.at[m, v], ret_r.at[m, v])
        for q in range(blocks):
            cols = slice(q * BLOCK, (q + 1) * BLOCK)
            found = jnp.dot(whole_ref[m], ret_ref[m, :, cols], preferred_element_type=F32)
            found += jnp.dot(split_ref[m, q], ret_ref[m, :, width:], preferred_element_type=F32)
            out_ref[m, :, cols] = found.astype(BF16)
        for copy in backs[m]:
            copy.wait_send()


def write_kernel(both, out_fwd, out_bwd, sems):
    odd = lax.rem(lax.axis_index("section"), 2)
    stores = [
        pltpu.make_async_copy(both.at[1 - odd], out_fwd, sems.at[0]),
        pltpu.make_async_copy(both.at[odd], out_bwd, sems.at[1]),
    ]
    for store in stores:
        store.start()
    for store in stores:
        store.wait()


def on_device(sent_fwd, sent_bwd, router_w, w_up, w_down, routes_fwd, routes_bwd):
    tokens, width = sent_fwd.shape[1:]
    hidden = w_up.shape[2]
    experts = router_w.shape[2]
    sections = lax.axis_size("section")
    chips = lax.axis_size("expert") // 2
    per_expert = chips // experts
    dims = (chips, per_expert, experts, sections, tokens, width, hidden)
    chunks = width // CHUNK
    wide = width + BLOCK
    main = chips * BASE
    half = main + -(-chips // 16) * 16
    dma = pltpu.SemaphoreType.DMA
    hbm = pl.BlockSpec(memory_space=pltpu.HBM)
    vmem = pl.BlockSpec(memory_space=pltpu.VMEM)
    shape = jax.ShapeDtypeStruct((tokens, width), BF16)
    assert sections % 2 == 0 and sections > 2
    both = pl.pallas_call(
        functools.partial(layer_kernel, dims),
        out_shape=jax.ShapeDtypeStruct((2, tokens, width), BF16),
        in_specs=[hbm] * 7,
        out_specs=vmem,
        scratch_shapes=[
            pltpu.VMEM((2, tokens, width), BF16),
            pltpu.VMEM((2, 2 * half, wide), BF16),
            pltpu.VMEM((2, experts * BASE, wide), BF16),
            pltpu.VMEM((width, hidden), BF16),
            pltpu.VMEM((hidden, width), BF16),
            pltpu.VMEM((2, 2 * half, hidden), BF16),
            pltpu.VMEM((experts, width), F32),
            pltpu.VMEM((2, 1, tokens), jnp.int32),
            pltpu.VMEM((2, 1, tokens), jnp.int32),
            pltpu.VMEM((2, 1, tokens), jnp.int32),
            pltpu.VMEM((2, chunks, half, CHUNK), BF16),
            pltpu.VMEM((2, chunks, half, CHUNK), BF16),
            pltpu.VMEM((chunks, half, CHUNK), BF16),
            pltpu.VMEM((2, main, wide), BF16),
            pltpu.VMEM((2, main, wide), BF16),
            pltpu.VMEM((2, tokens, main), BF16),
            pltpu.VMEM((2, width // BLOCK, tokens, main), BF16),
            dma((5,)), dma((2,)), dma((2,)), dma((2,)),
            dma((2, chips)), dma((2, chips)),
            dma((2, chips)), dma((2, chips)),
            dma((2, chunks)), dma((2, chunks)),
            dma((2, chips)), dma((2, chips)), dma((2,)),
            pltpu.SemaphoreType.REGULAR((2,)), pltpu.SemaphoreType.REGULAR((2,)), pltpu.SemaphoreType.REGULAR((1,)),
        ],
        compiler_params=pltpu.CompilerParams(
            collective_id=0, has_side_effects=True, vmem_limit_bytes=40 << 20
        ),
    )(
        *[pltpu.with_memory_space_constraint(given, pltpu.HBM) for given in (
            routes_fwd.reshape(1, tokens), routes_bwd.reshape(1, tokens),
            sent_fwd[0], sent_bwd[0], router_w[0].T, w_up[0], w_down[0],
        )]
    )
    out_fwd, out_bwd = pl.pallas_call(
        write_kernel,
        out_shape=(shape, shape),
        in_specs=[vmem],
        out_specs=(hbm, hbm),
        scratch_shapes=[dma((2,))],
        compiler_params=pltpu.CompilerParams(has_side_effects=True, vmem_limit_bytes=8 << 20),
    )(both)
    return out_fwd[None], out_bwd[None]


def solution(mesh):
    return jax.shard_map(
        on_device,
        mesh=mesh,
        in_specs=(
            P("section", "expert", None),
            P("section", "expert", None),
            P("section", None, None),
            P("section", None, "expert"),
            P("section", "expert", None),
            P("section", "expert", None),
            P("section", "expert", None),
        ),
        out_specs=(P("section", "expert", None), P("section", "expert", None)),
        check_vma=False,
    )
```

```python
import functools

import jax
import jax.numpy as jnp
from jax import lax
from jax.experimental import pallas as pl
from jax.experimental.pallas import tpu as pltpu
from jax.sharding import PartitionSpec as P

MESH = pl.DeviceIdType.MESH
F32 = jnp.float32
BF16 = jnp.bfloat16
NT = (((1,), (1,)), ((), ()))
BASE = 16
BLOCK = 256
CHUNK = 512


def iota(shape, dim):
    return lax.broadcasted_iota(jnp.int32, shape, dim)


def ones_where(mask):
    return jnp.where(mask, 1.0, 0.0).astype(BF16)


def exact(a, b):
    return jnp.dot(a, b, preferred_element_type=F32).astype(BF16)


def to_blocks(rows, number):
    height = rows[0].shape[0]
    i, j = iota((number * 16, len(rows) * height), 0), iota((number * 16, len(rows) * height), 1)
    take = ones_where(j == (i % 16) * height + i // 16)
    return exact(take, jnp.concatenate(rows, axis=0))


def from_blocks(blocks, number, height):
    n = blocks.shape[0]
    i, j = iota((number * height, n), 0), iota((number * height, n), 1)
    take = ones_where(i == (j % 16) * height + j // 16)
    rows = exact(take, blocks)
    return [rows[q * height:(q + 1) * height] for q in range(number)]


def positions(chosen, experts):
    tokens = chosen.shape[1]
    named = iota((16, tokens), 0) == chosen
    earlier = ones_where(iota((tokens, tokens), 0) < iota((tokens, tokens), 1))
    counted = jnp.dot(ones_where(named), earlier, preferred_element_type=F32)
    place = jnp.sum(jnp.where(named, counted, 0.0), axis=0, keepdims=True)
    return place.astype(jnp.int32)


def slots(chosen, experts):
    place = positions(chosen, experts)
    return jnp.where(place < BASE, chosen * BASE + place, experts * BASE + chosen)


def unpacked(ret, whole, split, q):
    width = ret.shape[1] - BLOCK
    found = jnp.dot(whole[...], ret[:, q * BLOCK:(q + 1) * BLOCK], preferred_element_type=F32)
    found += jnp.dot(split[q], ret[:, width:], preferred_element_type=F32)
    return found.astype(BF16)


def layer_kernel(
    dims,
    rf_hbm, rb_hbm, fwd_hbm, bwd_hbm, router_hbm, up_hbm, down_hbm,
    out_ref, last_ret, last_whole, last_split,
    x_ref, rows_ref, pack_ref, up_ref, down_ref, hid_ref, router_ref, routes_ref, slot_ref, next_slots,
    part_out, part_in, own_part, y_ref, ret_ref, whole_ref, split_ref,
    load_s, w_s, small_s, small_r, disp_s, disp_r, pair_s, pair_r, part_s, part_r, ret_s, ret_r, loc_s, chain, far, hop,
):
    chips, per_expert, experts, sections, tokens, width, hidden = dims
    blocks = width // BLOCK
    chunks = width // CHUNK
    main = chips * BASE
    spare = -(-chips // 16) * 16
    half = main + spare
    section = lax.axis_index("section")
    me = lax.axis_index("expert")
    core = lax.rem(me, 2)
    chip = me // 2
    sib = {"section": section, "expert": chip * 2 + 1 - core}
    odd = lax.rem(section, 2)
    there = (section + 1 - 2 * odd, lax.rem(section + sections - 1 + 2 * odd, sections))
    informer = lax.rem(section + sections - 2 + 4 * odd, sections)
    informed = lax.rem(section + sections + 2 - 4 * odd, sections)

    def partner(v):
        other, bit = chip, 1
        while bit <= v:
            if (v // bit) % 2:
                other = other + bit - 2 * bit * lax.rem(chip // bit, 2)
            bit *= 2
        return other

    def beside(v):
        return (partner(v) == chip + 1) | (partner(v) == chip - 1)

    order = [v for v in range(chips // 2, chips)] + [v for v in range(1, chips // 2)] + [0]

    def remote(src, dst, send, recv, device):
        return pltpu.make_async_remote_copy(
            src_ref=src, dst_ref=dst, send_sem=send, recv_sem=recv,
            device_id=device, device_id_type=MESH,
        )

    def arrived(dst, send, recv):
        remote(dst, dst, send, recv, sib).wait_recv()

    above = {"section": section, "expert": me + 2}
    below = {"section": section, "expert": me - 2}

    def signal(semaphore, device):
        pl.semaphore_signal(semaphore, inc=1, device_id=device, device_id_type=MESH)

    barrier = pltpu.get_barrier_semaphore()
    signal(barrier, {"section": there[0], "expert": me})
    signal(barrier, {"section": informer, "expert": me})
    signal(barrier, sib)

    @pl.when(chip > 0)
    def _():
        signal(barrier, below)

    @pl.when(chip < chips - 1)
    def _():
        signal(barrier, above)

    def loads_of(flip):
        routes, sent = (rb_hbm, rf_hbm), (fwd_hbm, bwd_hbm)
        return [
            pltpu.make_async_copy(routes[flip], routes_ref.at[0], load_s.at[0]),
            pltpu.make_async_copy(routes[1 - flip], routes_ref.at[1], load_s.at[1]),
            pltpu.make_async_copy(sent[flip], x_ref.at[0], load_s.at[2]),
            pltpu.make_async_copy(sent[1 - flip], x_ref.at[1], load_s.at[3]),
        ]

    for flip in range(2):
        @pl.when(odd == flip)
        def _():
            for load in loads_of(flip):
                load.start()

    loads = loads_of(0) + [pltpu.make_async_copy(router_hbm, router_ref, load_s.at[4])]
    loads[4].start()
    w_up_copy = pltpu.make_async_copy(up_hbm, up_ref, w_s.at[0])
    w_down_copy = pltpu.make_async_copy(down_hbm, down_ref, w_s.at[1])
    for m in range(2):
        loads[m].wait()
        slot_ref[m] = slots(routes_ref[m], experts)
    pl.semaphore_wait(barrier, 3 + jnp.where(chip > 0, 1, 0) + jnp.where(chip < chips - 1, 1, 0))

    sends = []

    backs = ([], [])
    rets, wholes, splits = (ret_ref, last_ret), (whole_ref, last_whole), (split_ref, last_split)

    def send(*args):
        copy = remote(*args)
        copy.start()
        sends.append(copy)

    def back(m, *args):
        copy = remote(*args)
        copy.start()
        backs[m].append(copy)

    def send_slots(m):
        send(slot_ref.at[m], next_slots.at[m], small_s.at[m], small_r.at[m], {"section": there[m], "expert": me})

    send_slots(0)
    signal(hop.at[0], {"section": informed, "expert": me})

    @pl.when(chip == 1)
    def _():
        signal(chain.at[0], above)

    @pl.when(chip == chips - 2)
    def _():
        signal(chain.at[1], below)

    def finish_chain():
        @pl.when(chip >= 2)
        def _():
            pl.semaphore_wait(chain.at[0], 1)

        @pl.when((chip >= 2) & (chip <= chips - 2))
        def _():
            signal(chain.at[0], above)

        @pl.when(chip <= chips - 3)
        def _():
            pl.semaphore_wait(chain.at[1], 1)

        @pl.when((chip >= 1) & (chip <= chips - 3))
        def _():
            signal(chain.at[1], below)

        signal(far.at[0], {"section": there[0], "expert": me})
        signal(far.at[1], {"section": there[1], "expert": me})

    for m in range(2):
        loads[2 + m].wait()
        arrived(next_slots.at[m], small_s.at[m], small_r.at[m])
        take = ones_where(iota((experts * BASE + 16, tokens), 0) == next_slots[m])
        extra = []
        for k in range(chunks):
            packed = exact(take, x_ref[m, :, k * CHUNK:(k + 1) * CHUNK])
            pack_ref[m, :, k * CHUNK:(k + 1) * CHUNK] = packed[0:experts * BASE]
            for b in range(CHUNK // BLOCK):
                extra.append(packed[experts * BASE:, b * BLOCK:(b + 1) * BLOCK])
        pack_ref[m, :, width:] = to_blocks(extra, experts)
        copies = {}
        for v in order:
            other = partner(v)
            copies[v] = remote(
                pack_ref.at[m, pl.ds(pl.multiple_of(other // per_expert * BASE, BASE), BASE), :],
                rows_ref.at[m, pl.ds(v * BASE, BASE), :],
                disp_s.at[m, v], disp_r.at[m, v],
                {"section": there[m], "expert": other * 2 + core},
            )
            sends.append(copies[v])
        if m == 0:
            pl.semaphore_wait(hop.at[0], 1)
            send_slots(1)
        for v in order:
            if m == 0 and v > 1 and v & (v + 1) == 0:
                pl.when(beside(v))(copies[v].start)
        if m == 0:
            finish_chain()
            w_up_copy.start()
            w_down_copy.start()
        pl.semaphore_wait(far.at[m], 1)
        for v in order:
            if m == 0 and v > 1 and v & (v + 1) == 0:
                pl.when(jnp.logical_not(beside(v)))(copies[v].start)
            else:
                copies[v].start()

    loads[4].wait()
    expert = chip // per_expert
    column = jnp.where(iota((experts, width), 0) == expert, router_ref[...], 0.0)
    column = jnp.sum(column, axis=0, keepdims=True)
    w_up_copy.wait()
    w_down_copy.wait()

    eye = ones_where(iota((tokens, tokens), 0) == iota((tokens, tokens), 1))
    lane = iota((tokens, main), 1)
    within, expert_of = lane % BASE, lane // (BASE * per_expert)
    for m in range(2):
        slot = jnp.broadcast_to(slot_ref[m].astype(F32), (8, tokens)).astype(BF16)
        slot = lax.dot_general(eye, slot, NT, preferred_element_type=F32)[:, 0:1].astype(jnp.int32)
        wholes[m][...] = ones_where(expert_of * BASE + within == slot)
        split = expert_of + experts * BASE == slot
        for q in range(blocks):
            splits[m][q] = ones_where(split & (within == q))

    for m in range(2):
        for v in order:
            mine = rows_ref.at[m, pl.ds(v * BASE, BASE), :]
            arrived(mine, disp_s.at[m, v], disp_r.at[m, v])
            send(mine, rows_ref.at[m, pl.ds(half + v * BASE, BASE), :], pair_s.at[m, v], pair_r.at[m, v], sib)

        def spread(start):
            found = from_blocks(rows_ref[m, start:start + main, width:], blocks, spare)
            for q in range(blocks):
                rows_ref[m, start + main:start + half, q * BLOCK:(q + 1) * BLOCK] = found[q]

        spread(0)
        total = jnp.zeros((half, 128), F32)
        for b in range(width // 128):
            cols = slice(b * 128, (b + 1) * 128)
            total += rows_ref[m, 0:half, cols].astype(F32) * column[:, cols]
        score = jax.nn.sigmoid(jnp.sum(total, axis=1, keepdims=True))
        first = lax.rem(chip, per_expert) == 0

        for v in order:
            arrived(rows_ref.at[m, pl.ds(half + v * BASE, BASE), :], pair_s.at[m, v], pair_r.at[m, v])
        spread(half)
        hid_ref[m] = jax.nn.silu(
            jnp.dot(rows_ref[m, :, 0:width], up_ref[...], preferred_element_type=F32)
        ).astype(BF16)

        for k in range(chunks):
            part = exact(hid_ref[m], down_ref[:, k * CHUNK:(k + 1) * CHUNK])
            part_out[m, k] = part[half:]
            own_part[k] = part[0:half]
            send(part_out.at[m, k], part_in.at[m, k], part_s.at[m, k], part_r.at[m, k], sib)
        extra = []
        for k in range(chunks):
            arrived(part_in.at[m, k], part_s.at[m, k], part_r.at[m, k])
            added = score * (own_part[k].astype(F32) + part_in[m, k].astype(F32))
            x = rows_ref[m, 0:half, k * CHUNK:(k + 1) * CHUNK].astype(F32)
            if per_expert > 1:
                x = jnp.where(first, x, 0.0)
            y = (x + added).astype(BF16)
            y_ref[m, :, k * CHUNK:(k + 1) * CHUNK] = y[0:main]
            for b in range(CHUNK // BLOCK):
                extra.append(y[main:, b * BLOCK:(b + 1) * BLOCK])
        y_ref[m, :, width:] = to_blocks(extra, chips)
        for v in order:
            y = y_ref.at[m, pl.ds(v * BASE, BASE), :]
            home = rets[m].at[pl.ds(pl.multiple_of(chip * BASE, BASE), BASE), :]
            if v == 0:
                pltpu.make_async_copy(y, home, loc_s.at[m]).start()
            else:
                back(m, y, home, ret_s.at[m, v], ret_r.at[m, v], {"section": section, "expert": partner(v) * 2 + core})

    for copy in sends:
        copy.wait_send()
    for m in range(2):
        for v in order:
            here = rets[m].at[pl.ds(pl.multiple_of(partner(v) * BASE, BASE), BASE), :]
            if v == 0:
                pltpu.make_async_copy(here, here, loc_s.at[m]).wait()
            else:
                arrived(here, ret_s.at[m, v], ret_r.at[m, v])
        if m == 0:
            for q in range(blocks):
                out_ref[:, q * BLOCK:(q + 1) * BLOCK] = unpacked(ret_ref, whole_ref, split_ref, q)
        for copy in backs[m]:
            copy.wait_send()


def write_kernel(first, ret, whole, split, out_fwd, out_bwd, held, sems):
    odd = lax.rem(lax.axis_index("section"), 2)
    blocks = split.shape[0]
    half = -(-blocks // 2)
    pieces = [(0, half * BLOCK), (half * BLOCK, (blocks - half) * BLOCK)]

    def copy(src, n, flip, chunk):
        start, size = pieces[n]
        cols = pl.ds(start, size)
        out = out_bwd if flip == chunk else out_fwd
        return pltpu.make_async_copy(src.at[:, cols], out.at[:, cols], sems.at[chunk, n])

    def start(src, n, chunk):
        for flip in range(2):
            pl.when(odd == flip)(copy(src, n, flip, chunk).start)

    for n in range(2):
        start(first, n, 0)
    for n, (begin, size) in enumerate(pieces):
        for q in range(begin // BLOCK, (begin + size) // BLOCK):
            held[:, q * BLOCK:(q + 1) * BLOCK] = unpacked(ret, whole, split, q)
        start(held, n, 1)
    for n in range(2):
        copy(first, n, 0, 0).wait()
        copy(held, n, 0, 1).wait()


def on_device(sent_fwd, sent_bwd, router_w, w_up, w_down, routes_fwd, routes_bwd):
    tokens, width = sent_fwd.shape[1:]
    hidden = w_up.shape[2]
    experts = router_w.shape[2]
    sections = lax.axis_size("section")
    chips = lax.axis_size("expert") // 2
    per_expert = chips // experts
    dims = (chips, per_expert, experts, sections, tokens, width, hidden)
    chunks = width // CHUNK
    wide = width + BLOCK
    main = chips * BASE
    half = main + -(-chips // 16) * 16
    dma = pltpu.SemaphoreType.DMA
    hbm = pl.BlockSpec(memory_space=pltpu.HBM)
    vmem = pl.BlockSpec(memory_space=pltpu.VMEM)
    shape = jax.ShapeDtypeStruct((tokens, width), BF16)
    assert sections % 2 == 0 and sections > 2
    results = pl.pallas_call(
        functools.partial(layer_kernel, dims),
        out_shape=(
            shape,
            jax.ShapeDtypeStruct((main, wide), BF16),
            jax.ShapeDtypeStruct((tokens, main), BF16),
            jax.ShapeDtypeStruct((width // BLOCK, tokens, main), BF16),
        ),
        in_specs=[hbm] * 7,
        out_specs=(vmem,) * 4,
        scratch_shapes=[
            pltpu.VMEM((2, tokens, width), BF16),
            pltpu.VMEM((2, 2 * half, wide), BF16),
            pltpu.VMEM((2, experts * BASE, wide), BF16),
            pltpu.VMEM((width, hidden), BF16),
            pltpu.VMEM((hidden, width), BF16),
            pltpu.VMEM((2, 2 * half, hidden), BF16),
            pltpu.VMEM((experts, width), F32),
            pltpu.VMEM((2, 1, tokens), jnp.int32),
            pltpu.VMEM((2, 1, tokens), jnp.int32),
            pltpu.VMEM((2, 1, tokens), jnp.int32),
            pltpu.VMEM((2, chunks, half, CHUNK), BF16),
            pltpu.VMEM((2, chunks, half, CHUNK), BF16),
            pltpu.VMEM((chunks, half, CHUNK), BF16),
            pltpu.VMEM((2, main, wide), BF16),
            pltpu.VMEM((main, wide), BF16),
            pltpu.VMEM((tokens, main), BF16),
            pltpu.VMEM((width // BLOCK, tokens, main), BF16),
            dma((5,)), dma((2,)), dma((2,)), dma((2,)),
            dma((2, chips)), dma((2, chips)),
            dma((2, chips)), dma((2, chips)),
            dma((2, chunks)), dma((2, chunks)),
            dma((2, chips)), dma((2, chips)), dma((2,)),
            pltpu.SemaphoreType.REGULAR((2,)), pltpu.SemaphoreType.REGULAR((2,)), pltpu.SemaphoreType.REGULAR((1,)),
        ],
        compiler_params=pltpu.CompilerParams(
            collective_id=0, has_side_effects=True, vmem_limit_bytes=40 << 20
        ),
    )(
        *[pltpu.with_memory_space_constraint(given, pltpu.HBM) for given in (
            routes_fwd.reshape(1, tokens), routes_bwd.reshape(1, tokens),
            sent_fwd[0], sent_bwd[0], router_w[0].T, w_up[0], w_down[0],
        )]
    )
    out_fwd, out_bwd = pl.pallas_call(
        write_kernel,
        out_shape=(shape, shape),
        in_specs=[vmem] * 4,
        out_specs=(hbm, hbm),
        scratch_shapes=[pltpu.VMEM((tokens, width), BF16), dma((2, 2))],
        compiler_params=pltpu.CompilerParams(has_side_effects=True, vmem_limit_bytes=8 << 20),
    )(*results)
    return out_fwd[None], out_bwd[None]


def solution(mesh):
    return jax.shard_map(
        on_device,
        mesh=mesh,
        in_specs=(
            P("section", "expert", None),
            P("section", "expert", None),
            P("section", None, None),
            P("section", None, "expert"),
            P("section", "expert", None),
            P("section", "expert", None),
            P("section", "expert", None),
        ),
        out_specs=(P("section", "expert", None), P("section", "expert", None)),
        check_vma=False,
    )
```

```python
import functools

import jax
import jax.numpy as jnp
from jax import lax
from jax.experimental import pallas as pl
from jax.experimental.pallas import tpu as pltpu
from jax.sharding import PartitionSpec as P

MESH = pl.DeviceIdType.MESH
F32 = jnp.float32
BF16 = jnp.bfloat16
NT = (((1,), (1,)), ((), ()))
BASE = 16
BLOCK = 256
CHUNK = 512


def iota(shape, dim):
    return lax.broadcasted_iota(jnp.int32, shape, dim)


def ones_where(mask):
    return jnp.where(mask, 1.0, 0.0).astype(BF16)


def exact(a, b):
    return jnp.dot(a, b, preferred_element_type=F32).astype(BF16)


def to_blocks(rows, number):
    height = rows[0].shape[0]
    i, j = iota((number * 16, len(rows) * height), 0), iota((number * 16, len(rows) * height), 1)
    take = ones_where(j == (i % 16) * height + i // 16)
    return exact(take, jnp.concatenate(rows, axis=0))


def from_blocks(blocks, number, height):
    n = blocks.shape[0]
    i, j = iota((number * height, n), 0), iota((number * height, n), 1)
    take = ones_where(i == (j % 16) * height + j // 16)
    rows = exact(take, blocks)
    return [rows[q * height:(q + 1) * height] for q in range(number)]


def positions(chosen, experts):
    tokens = chosen.shape[1]
    named = iota((16, tokens), 0) == chosen
    earlier = ones_where(iota((tokens, tokens), 0) < iota((tokens, tokens), 1))
    counted = jnp.dot(ones_where(named), earlier, preferred_element_type=F32)
    place = jnp.sum(jnp.where(named, counted, 0.0), axis=0, keepdims=True)
    return place.astype(jnp.int32)


def slots(chosen, experts):
    place = positions(chosen, experts)
    return jnp.where(place < BASE, chosen * BASE + place, experts * BASE + chosen)


def unpacked(ret, whole, split, q):
    width = ret.shape[1] - BLOCK
    found = jnp.dot(whole[...], ret[:, q * BLOCK:(q + 1) * BLOCK], preferred_element_type=F32)
    found += jnp.dot(split[q], ret[:, width:], preferred_element_type=F32)
    return found.astype(BF16)


def layer_kernel(
    dims,
    rf_hbm, rb_hbm, fwd_hbm, bwd_hbm, router_hbm, up_hbm, down_hbm,
    out_ref, last_ret, last_whole, last_split,
    x_ref, rows_ref, pack_ref, up_ref, down_ref, hid_ref, router_ref, routes_ref, slot_ref, next_slots,
    part_out, part_in, own_part, y_ref, ret_ref, whole_ref, split_ref,
    load_s, w_s, small_s, small_r, disp_s, disp_r, pair_s, pair_r, part_s, part_r, ret_s, ret_r, loc_s, chain, far, hop,
):
    chips, per_expert, experts, sections, tokens, width, hidden = dims
    blocks = width // BLOCK
    chunks = width // CHUNK
    main = chips * BASE
    spare = -(-chips // 16) * 16
    half = main + spare
    section = lax.axis_index("section")
    me = lax.axis_index("expert")
    core = lax.rem(me, 2)
    chip = me // 2
    sib = {"section": section, "expert": chip * 2 + 1 - core}
    odd = lax.rem(section, 2)
    there = (section + 1 - 2 * odd, lax.rem(section + sections - 1 + 2 * odd, sections))
    informer = lax.rem(section + sections - 2 + 4 * odd, sections)
    informed = lax.rem(section + sections + 2 - 4 * odd, sections)

    def partner(v):
        other, bit = chip, 1
        while bit <= v:
            if (v // bit) % 2:
                other = other + bit - 2 * bit * lax.rem(chip // bit, 2)
            bit *= 2
        return other

    def beside(v):
        return (partner(v) == chip + 1) | (partner(v) == chip - 1)

    order = [v for v in range(chips // 2, chips)] + [v for v in range(1, chips // 2)] + [0]

    def remote(src, dst, send, recv, device):
        return pltpu.make_async_remote_copy(
            src_ref=src, dst_ref=dst, send_sem=send, recv_sem=recv,
            device_id=device, device_id_type=MESH,
        )

    def arrived(dst, send, recv):
        remote(dst, dst, send, recv, sib).wait_recv()

    above = {"section": section, "expert": me + 2}
    below = {"section": section, "expert": me - 2}

    def signal(semaphore, device):
        pl.semaphore_signal(semaphore, inc=1, device_id=device, device_id_type=MESH)

    barrier = pltpu.get_barrier_semaphore()
    signal(barrier, {"section": there[0], "expert": me})
    signal(barrier, {"section": informer, "expert": me})
    signal(barrier, sib)

    @pl.when(chip > 0)
    def _():
        signal(barrier, below)

    @pl.when(chip < chips - 1)
    def _():
        signal(barrier, above)

    def loads_of(flip):
        routes, sent = (rb_hbm, rf_hbm), (fwd_hbm, bwd_hbm)
        return [
            pltpu.make_async_copy(routes[flip], routes_ref.at[0], load_s.at[0]),
            pltpu.make_async_copy(routes[1 - flip], routes_ref.at[1], load_s.at[1]),
            pltpu.make_async_copy(sent[flip], x_ref.at[0], load_s.at[2]),
            pltpu.make_async_copy(sent[1 - flip], x_ref.at[1], load_s.at[3]),
        ]

    for flip in range(2):
        @pl.when(odd == flip)
        def _():
            for load in loads_of(flip):
                load.start()

    loads = loads_of(0) + [pltpu.make_async_copy(router_hbm, router_ref, load_s.at[4])]
    loads[4].start()
    w_up_copy = pltpu.make_async_copy(up_hbm, up_ref, w_s.at[0])
    w_down_copy = pltpu.make_async_copy(down_hbm, down_ref, w_s.at[1])
    for m in range(2):
        loads[m].wait()
        slot_ref[m] = slots(routes_ref[m], experts)
    pl.semaphore_wait(barrier, 3 + jnp.where(chip > 0, 1, 0) + jnp.where(chip < chips - 1, 1, 0))

    sends = []

    backs = ([], [])
    rets, wholes, splits = (ret_ref, last_ret), (whole_ref, last_whole), (split_ref, last_split)

    def send(*args):
        copy = remote(*args)
        copy.start()
        sends.append(copy)

    def back(m, *args):
        copy = remote(*args)
        copy.start()
        backs[m].append(copy)

    def send_slots(m):
        send(slot_ref.at[m], next_slots.at[m], small_s.at[m], small_r.at[m], {"section": there[m], "expert": me})

    send_slots(0)
    signal(hop.at[0], {"section": informed, "expert": me})

    @pl.when(chip == 1)
    def _():
        signal(chain.at[0], above)

    @pl.when(chip == chips - 2)
    def _():
        signal(chain.at[1], below)

    def finish_chain():
        @pl.when(chip >= 2)
        def _():
            pl.semaphore_wait(chain.at[0], 1)

        @pl.when((chip >= 2) & (chip <= chips - 2))
        def _():
            signal(chain.at[0], above)

        @pl.when(chip <= chips - 3)
        def _():
            pl.semaphore_wait(chain.at[1], 1)

        @pl.when((chip >= 1) & (chip <= chips - 3))
        def _():
            signal(chain.at[1], below)

        signal(far.at[0], {"section": there[0], "expert": me})
        signal(far.at[1], {"section": there[1], "expert": me})

    for m in range(2):
        loads[2 + m].wait()
        arrived(next_slots.at[m], small_s.at[m], small_r.at[m])
        take = ones_where(iota((experts * BASE + 16, tokens), 0) == next_slots[m])
        extra = []
        for k in range(chunks):
            packed = exact(take, x_ref[m, :, k * CHUNK:(k + 1) * CHUNK])
            pack_ref[m, :, k * CHUNK:(k + 1) * CHUNK] = packed[0:experts * BASE]
            for b in range(CHUNK // BLOCK):
                extra.append(packed[experts * BASE:, b * BLOCK:(b + 1) * BLOCK])
        pack_ref[m, :, width:] = to_blocks(extra, experts)
        copies = {}
        for v in order:
            other = partner(v)
            copies[v] = remote(
                pack_ref.at[m, pl.ds(pl.multiple_of(other // per_expert * BASE, BASE), BASE), :],
                rows_ref.at[m, pl.ds(v * BASE, BASE), :],
                disp_s.at[m, v], disp_r.at[m, v],
                {"section": there[m], "expert": other * 2 + core},
            )
            sends.append(copies[v])
        if m == 0:
            pl.semaphore_wait(hop.at[0], 1)
            send_slots(1)
        for v in order:
            if m == 0 and v > 1 and v & (v + 1) == 0:
                pl.when(beside(v))(copies[v].start)
        if m == 0:
            finish_chain()
            w_up_copy.start()
            w_down_copy.start()
        pl.semaphore_wait(far.at[m], 1)
        for v in order:
            if m == 0 and v > 1 and v & (v + 1) == 0:
                pl.when(jnp.logical_not(beside(v)))(copies[v].start)
            else:
                copies[v].start()

    loads[4].wait()
    expert = chip // per_expert
    column = jnp.where(iota((experts, width), 0) == expert, router_ref[...], 0.0)
    column = jnp.sum(column, axis=0, keepdims=True)
    w_up_copy.wait()
    w_down_copy.wait()

    eye = ones_where(iota((tokens, tokens), 0) == iota((tokens, tokens), 1))
    lane = iota((tokens, main), 1)
    within, expert_of = lane % BASE, lane // (BASE * per_expert)
    for m in range(2):
        slot = jnp.broadcast_to(slot_ref[m].astype(F32), (8, tokens)).astype(BF16)
        slot = lax.dot_general(eye, slot, NT, preferred_element_type=F32)[:, 0:1].astype(jnp.int32)
        wholes[m][...] = ones_where(expert_of * BASE + within == slot)
        split = expert_of + experts * BASE == slot
        for q in range(blocks):
            splits[m][q] = ones_where(split & (within == q))

    for m in range(2):
        for v in order:
            mine = rows_ref.at[m, pl.ds(v * BASE, BASE), :]
            arrived(mine, disp_s.at[m, v], disp_r.at[m, v])
            send(mine, rows_ref.at[m, pl.ds(half + v * BASE, BASE), :], pair_s.at[m, v], pair_r.at[m, v], sib)

        def spread(start):
            found = from_blocks(rows_ref[m, start:start + main, width:], blocks, spare)
            for q in range(blocks):
                rows_ref[m, start + main:start + half, q * BLOCK:(q + 1) * BLOCK] = found[q]

        spread(0)
        total = jnp.zeros((half, 128), F32)
        for b in range(width // 128):
            cols = slice(b * 128, (b + 1) * 128)
            total += rows_ref[m, 0:half, cols].astype(F32) * column[:, cols]
        score = jax.nn.sigmoid(jnp.sum(total, axis=1, keepdims=True))
        first = lax.rem(chip, per_expert) == 0

        for v in order:
            arrived(rows_ref.at[m, pl.ds(half + v * BASE, BASE), :], pair_s.at[m, v], pair_r.at[m, v])
        spread(half)
        hid_ref[m] = jax.nn.silu(
            jnp.dot(rows_ref[m, :, 0:width], up_ref[...], preferred_element_type=F32)
        ).astype(BF16)

        for k in range(chunks):
            part = exact(hid_ref[m], down_ref[:, k * CHUNK:(k + 1) * CHUNK])
            part_out[m, k] = part[half:]
            own_part[k] = part[0:half]
            send(part_out.at[m, k], part_in.at[m, k], part_s.at[m, k], part_r.at[m, k], sib)
        extra = []
        for k in range(chunks):
            arrived(part_in.at[m, k], part_s.at[m, k], part_r.at[m, k])
            added = score * (own_part[k].astype(F32) + part_in[m, k].astype(F32))
            x = rows_ref[m, 0:half, k * CHUNK:(k + 1) * CHUNK].astype(F32)
            if per_expert > 1:
                x = jnp.where(first, x, 0.0)
            y = (x + added).astype(BF16)
            y_ref[m, :, k * CHUNK:(k + 1) * CHUNK] = y[0:main]
            for b in range(CHUNK // BLOCK):
                extra.append(y[main:, b * BLOCK:(b + 1) * BLOCK])
        y_ref[m, :, width:] = to_blocks(extra, chips)
        for v in order:
            y = y_ref.at[m, pl.ds(v * BASE, BASE), :]
            home = rets[m].at[pl.ds(pl.multiple_of(chip * BASE, BASE), BASE), :]
            if v == 0:
                pltpu.make_async_copy(y, home, loc_s.at[m]).start()
            else:
                back(m, y, home, ret_s.at[m, v], ret_r.at[m, v], {"section": section, "expert": partner(v) * 2 + core})

    for copy in sends:
        copy.wait_send()
    for m in range(2):
        for v in order:
            here = rets[m].at[pl.ds(pl.multiple_of(partner(v) * BASE, BASE), BASE), :]
            if v == 0:
                pltpu.make_async_copy(here, here, loc_s.at[m]).wait()
            else:
                arrived(here, ret_s.at[m, v], ret_r.at[m, v])
        if m == 0:
            for q in range(blocks):
                out_ref[:, q * BLOCK:(q + 1) * BLOCK] = unpacked(ret_ref, whole_ref, split_ref, q)
        for copy in backs[m]:
            copy.wait_send()


def write_kernel(first, ret, whole, split, out_fwd, out_bwd, held, sems):
    odd = lax.rem(lax.axis_index("section"), 2)
    blocks = split.shape[0]
    cuts = [blocks * i // 4 * BLOCK for i in range(4 + 1)]
    pieces = [(a, b - a) for a, b in zip(cuts, cuts[1:])]

    def copy(src, n, flip, chunk):
        start, size = pieces[n]
        cols = pl.ds(start, size)
        out = out_bwd if flip == chunk else out_fwd
        return pltpu.make_async_copy(src.at[:, cols], out.at[:, cols], sems.at[chunk, n])

    def start(src, n, chunk):
        for flip in range(2):
            pl.when(odd == flip)(copy(src, n, flip, chunk).start)

    for n in range(len(pieces)):
        start(first, n, 0)
    for n, (begin, size) in enumerate(pieces):
        for q in range(begin // BLOCK, (begin + size) // BLOCK):
            held[:, q * BLOCK:(q + 1) * BLOCK] = unpacked(ret, whole, split, q)
        start(held, n, 1)
    for n in range(len(pieces)):
        copy(first, n, 0, 0).wait()
        copy(held, n, 0, 1).wait()


def on_device(sent_fwd, sent_bwd, router_w, w_up, w_down, routes_fwd, routes_bwd):
    tokens, width = sent_fwd.shape[1:]
    hidden = w_up.shape[2]
    experts = router_w.shape[2]
    sections = lax.axis_size("section")
    chips = lax.axis_size("expert") // 2
    per_expert = chips // experts
    dims = (chips, per_expert, experts, sections, tokens, width, hidden)
    chunks = width // CHUNK
    wide = width + BLOCK
    main = chips * BASE
    half = main + -(-chips // 16) * 16
    dma = pltpu.SemaphoreType.DMA
    hbm = pl.BlockSpec(memory_space=pltpu.HBM)
    vmem = pl.BlockSpec(memory_space=pltpu.VMEM)
    shape = jax.ShapeDtypeStruct((tokens, width), BF16)
    assert sections % 2 == 0 and sections > 2
    results = pl.pallas_call(
        functools.partial(layer_kernel, dims),
        out_shape=(
            shape,
            jax.ShapeDtypeStruct((main, wide), BF16),
            jax.ShapeDtypeStruct((tokens, main), BF16),
            jax.ShapeDtypeStruct((width // BLOCK, tokens, main), BF16),
        ),
        in_specs=[hbm] * 7,
        out_specs=(vmem,) * 4,
        scratch_shapes=[
            pltpu.VMEM((2, tokens, width), BF16),
            pltpu.VMEM((2, 2 * half, wide), BF16),
            pltpu.VMEM((2, experts * BASE, wide), BF16),
            pltpu.VMEM((width, hidden), BF16),
            pltpu.VMEM((hidden, width), BF16),
            pltpu.VMEM((2, 2 * half, hidden), BF16),
            pltpu.VMEM((experts, width), F32),
            pltpu.VMEM((2, 1, tokens), jnp.int32),
            pltpu.VMEM((2, 1, tokens), jnp.int32),
            pltpu.VMEM((2, 1, tokens), jnp.int32),
            pltpu.VMEM((2, chunks, half, CHUNK), BF16),
            pltpu.VMEM((2, chunks, half, CHUNK), BF16),
            pltpu.VMEM((chunks, half, CHUNK), BF16),
            pltpu.VMEM((2, main, wide), BF16),
            pltpu.VMEM((main, wide), BF16),
            pltpu.VMEM((tokens, main), BF16),
            pltpu.VMEM((width // BLOCK, tokens, main), BF16),
            dma((5,)), dma((2,)), dma((2,)), dma((2,)),
            dma((2, chips)), dma((2, chips)),
            dma((2, chips)), dma((2, chips)),
            dma((2, chunks)), dma((2, chunks)),
            dma((2, chips)), dma((2, chips)), dma((2,)),
            pltpu.SemaphoreType.REGULAR((2,)), pltpu.SemaphoreType.REGULAR((2,)), pltpu.SemaphoreType.REGULAR((1,)),
        ],
        compiler_params=pltpu.CompilerParams(
            collective_id=0, has_side_effects=True, vmem_limit_bytes=40 << 20
        ),
    )(
        *[pltpu.with_memory_space_constraint(given, pltpu.HBM) for given in (
            routes_fwd.reshape(1, tokens), routes_bwd.reshape(1, tokens),
            sent_fwd[0], sent_bwd[0], router_w[0].T, w_up[0], w_down[0],
        )]
    )
    out_fwd, out_bwd = pl.pallas_call(
        write_kernel,
        out_shape=(shape, shape),
        in_specs=[vmem] * 4,
        out_specs=(hbm, hbm),
        scratch_shapes=[pltpu.VMEM((tokens, width), BF16), dma((2, 4))],
        compiler_params=pltpu.CompilerParams(has_side_effects=True, vmem_limit_bytes=8 << 20),
    )(*results)
    return out_fwd[None], out_bwd[None]


def solution(mesh):
    return jax.shard_map(
        on_device,
        mesh=mesh,
        in_specs=(
            P("section", "expert", None),
            P("section", "expert", None),
            P("section", None, None),
            P("section", None, "expert"),
            P("section", "expert", None),
            P("section", "expert", None),
            P("section", "expert", None),
        ),
        out_specs=(P("section", "expert", None), P("section", "expert", None)),
        check_vma=False,
    )
```
